256 devices in a mesh: gx: 32 (over z, y), gy: 4 (over x_lo, core), pa: 2 (over x_hi).
Axes of the slice: x: 4 (x_hi: 2, x_lo: 2; x = x_hi * 2 + x_lo), y: 4, z: 8, core: 2. Of those that a mesh axis runs over, the one named last changes fastest.
Arguments:
- conductivity: float32 [256, 512, 256], P('gx', 'gy', 'pa'), may hold values from 0.5 to 1
- stored_state: bfloat16 [256, 512, 256], P('gx', 'gy', 'pa'), may hold values from -4 to 5
- row_scales: float32 [256, 512], P('gx', 'gy'), may hold values from 0.5 to 4
- cotangent: float32 [256, 512, 256], P('gx', 'gy', 'pa'), may hold values from -5 to 6
- upper_bound: float32 [1], replicated, may hold values from 97 to 145
Outputs:
- grad_conductivity: float32 [256, 512, 256], P('gx', 'gy', 'pa')
- adjoint: float32 [256, 512, 256], P('gx', 'gy', 'pa')
- state_new: float32 [256, 512, 256], P('gx', 'gy', 'pa')
- residuals: float32 [2, 256, 512, 256], P(None, 'gx', 'gy', 'pa')
The draws below stay inside these ranges and needn't reach their ends.
All inputs are finite; a program needn't handle non-finite values.
Results may differ from the reference program's by a relative error of at most 0.0003.
Values may be sent and summed in bfloat16 or wider, within the bound.
A program may use at most 128 MiB of HBM per device.

```python
import math
import jax
import jax.numpy as jnp

CZ = 128
CHEB = 16
NX = 256
NY = 512
NZ = 256


def smooth_pattern(shape_key):
    phases = jax.random.uniform(shape_key, (3,), jnp.float32, 0.0, 2.0 * math.pi)
    wave_first = jnp.cos(2.0 * math.pi * jnp.arange(NX, dtype=jnp.float32) / NX + phases[0])
    wave_second = jnp.cos(2.0 * math.pi * jnp.arange(NY, dtype=jnp.float32) / NY + phases[1])
    wave_third = jnp.cos(2.0 * math.pi * jnp.arange(NZ, dtype=jnp.float32) / NZ + phases[2])
    return wave_first[:, None, None] * wave_second[None, :, None] * wave_third[None, None, :]


def draw_stored_state(key, part):
    shape_key = jax.random.fold_in(key, 11)
    jitter_key = jax.random.fold_in(key, 12)
    pattern = smooth_pattern(shape_key)
    jitter = jax.random.normal(jitter_key, (NX, NY, NZ), jnp.float32)
    drawn = 1.0 + 0.4 * pattern + jitter
    return jnp.clip(drawn, -4.0, 5.0).astype(jnp.bfloat16)


def draw_cotangent(key, part):
    shape_key = jax.random.fold_in(key, 21)
    jitter_key = jax.random.fold_in(key, 22)
    pattern = smooth_pattern(shape_key)
    jitter = jax.random.normal(jitter_key, (NX, NY, NZ), jnp.float32)
    drawn = 0.8 + 0.3 * pattern + jitter
    return jnp.clip(drawn, -5.0, 6.0).astype(jnp.float32)


def level_of(key, dims, shards, least, largest):
    level, own = 1.0, jax.random.fold_in(key, 6)
    for position, blocks in shards:
        draws = jnp.exp(jax.random.uniform(jax.random.fold_in(own, position), (blocks,), jnp.float32, least / len(shards), largest / len(shards)))
        level = level * jnp.repeat(draws, dims[position] // blocks).reshape([-1 if axis == position else 1 for axis in range(len(dims))])
    return level


def setup_inputs(seed: int = 0) -> dict:
    splits = jax.random.split(jax.random.key(seed), 6)
    conductivity = jnp.clip(jnp.exp(math.log(1.0) - 0.6931472 * jax.random.uniform(splits[0], (NX, NY, NZ), jnp.float32) ** level_of(splits[0], (NX, NY, NZ), ((0, 32), (1, 4), (2, 2)), -0.2, 0.2)), 0.5, 1.0)
    stored_state = draw_stored_state(jax.random.fold_in(splits[5], 71), 0)
    row_scales = jnp.clip(jnp.exp(math.log(4.0) - 2.0794415 * jax.random.uniform(splits[2], (NX, NY), jnp.float32) ** level_of(splits[2], (NX, NY), ((0, 32), (1, 4)), -0.2, 0.2)), 0.5, 4.0)
    cotangent = draw_cotangent(jax.random.fold_in(splits[5], 71), 0)
    upper_bound = jnp.clip(jax.random.uniform(splits[4], (1,), jnp.float32, 97.0, 145.0), 97.0, 145.0)
    return {"conductivity": conductivity, "stored_state": stored_state, "row_scales": row_scales, "cotangent": cotangent, "upper_bound": upper_bound}


time_step = 8.0


def apply_operator(field, kappa):
    summed = jnp.zeros_like(field)
    for spatial in range(3):
        for shift in (1, -1):
            summed = summed + 0.5 * (kappa + jnp.roll(kappa, shift, spatial)) * (field - jnp.roll(field, shift, spatial))
    return field + time_step * summed


def chebyshev(rhs, kappa, upper):
    theta = 0.5 * (upper + 1.0)
    delta = 0.5 * (upper - 1.0)
    sigma = theta / delta
    rho = 1.0 / sigma
    solution = jnp.zeros_like(rhs)
    residual = rhs
    direction = rhs / theta
    for step in range(CHEB):
        solution = solution + direction
        residual = residual - apply_operator(direction, kappa)
        rho_next = 1.0 / (2.0 * sigma - rho)
        direction = rho_next * rho * direction + (2.0 * rho_next / delta) * residual
        rho = rho_next
    return solution, residual


def reference(conductivity, stored_state, row_scales, cotangent, upper_bound):
    upper = upper_bound[0]
    previous = jnp.roll(stored_state.astype(jnp.float32), CZ, 2) * row_scales[:, :, None]
    state_new, forward_res = chebyshev(previous, conductivity, upper)
    adjoint, adjoint_res = chebyshev(cotangent, conductivity, upper)
    summed = jnp.zeros_like(state_new)
    for spatial in range(3):
        for shift in (1, -1):
            summed = summed + (state_new - jnp.roll(state_new, shift, spatial)) * (adjoint - jnp.roll(adjoint, shift, spatial))
    grad_conductivity = -0.5 * time_step * summed
    return grad_conductivity, adjoint, state_new, jnp.stack((forward_res, adjoint_res))
```

```python
import jax
import jax.numpy as jnp
from jax import lax
from jax.sharding import PartitionSpec as P

CHEB = 16


time_step = 8.0


def ring(x, axis, step):
    count = lax.axis_size(axis)
    return lax.ppermute(x, axis, [(i, (i + step) % count) for i in range(count)])


def halos(cells):
    nd = cells.ndim
    dx, dy, dz = nd - 3, nd - 2, nd - 1
    x_lo = ring(lax.slice_in_dim(cells, cells.shape[dx] - 1, cells.shape[dx], axis=dx), "gx", 1)
    x_hi = ring(lax.slice_in_dim(cells, 0, 1, axis=dx), "gx", -1)
    y_lo = ring(lax.slice_in_dim(cells, cells.shape[dy] - 1, cells.shape[dy], axis=dy), "gy", 1)
    y_hi = ring(lax.slice_in_dim(cells, 0, 1, axis=dy), "gy", -1)
    ends = jnp.concatenate(
        [lax.slice_in_dim(cells, 0, 1, axis=dz), lax.slice_in_dim(cells, cells.shape[dz] - 1, cells.shape[dz], axis=dz)],
        axis=dz,
    )
    got = ring(ends, "pa", 1)
    z_lo = lax.slice_in_dim(got, 1, 2, axis=dz)
    z_hi = lax.slice_in_dim(got, 0, 1, axis=dz)
    return (x_lo, x_hi, y_lo, y_hi, z_lo, z_hi)


def neighbours(cells, faces):
    nd = cells.ndim
    out = []
    for k, dim in enumerate((nd - 3, nd - 2, nd - 1)):
        lo, hi = faces[2 * k], faces[2 * k + 1]
        n = cells.shape[dim]
        out.append(jnp.concatenate([lo, lax.slice_in_dim(cells, 0, n - 1, axis=dim)], axis=dim))
        out.append(jnp.concatenate([lax.slice_in_dim(cells, 1, n, axis=dim), hi], axis=dim))
    return out


def apply_operator(direction, weights):
    near = neighbours(direction, halos(direction))
    summed = jnp.zeros_like(direction)
    for w, n in zip(weights, near):
        summed = summed + w * (direction - n)
    return direction + summed


def body(conductivity, stored_state, row_scales, cotangent, upper_bound):
    upper = upper_bound[0]
    weights = [(conductivity + kn) * (0.5 * time_step) for kn in neighbours(conductivity, halos(conductivity))]
    partner = ring(stored_state, "pa", 1)
    previous = partner.astype(jnp.float32) * row_scales[:, :, None]
    rhs = jnp.stack((previous, cotangent))

    theta = 0.5 * (upper + 1.0)
    delta = 0.5 * (upper - 1.0)
    sigma = theta / delta
    rho = 1.0 / sigma
    start = (jnp.zeros_like(rhs), rhs, rhs / theta, rho)

    def sweep(step, carry):
        solution, residual, direction, rho_now = carry
        solution = solution + direction
        residual = residual - apply_operator(direction, weights)
        rho_next = 1.0 / (2.0 * sigma - rho_now)
        direction = rho_next * rho_now * direction + 2.0 * rho_next / delta * residual
        return (solution, residual, direction, rho_next)

    solved, residuals, _, _ = lax.fori_loop(0, CHEB, sweep, start)
    near = neighbours(solved, halos(solved))
    summed = jnp.zeros_like(solved[0])
    for n in near:
        differ = solved - n
        summed = summed + differ[0] * differ[1]
    grad_conductivity = -0.5 * time_step * summed
    return (grad_conductivity, solved[1], solved[0], residuals)


def solution(mesh):
    return jax.shard_map(
        body,
        mesh=mesh,
        in_specs=(
            P("gx", "gy", "pa"),
            P("gx", "gy", "pa"),
            P("gx", "gy"),
            P("gx", "gy", "pa"),
            P(),
        ),
        out_specs=(
            P("gx", "gy", "pa"),
            P("gx", "gy", "pa"),
            P("gx", "gy", "pa"),
            P(None, "gx", "gy", "pa"),
        ),
        check_vma=False,
    )
```

```python
import functools

import jax
import jax.numpy as jnp
from jax import lax
from jax.experimental import pallas as pl
from jax.experimental.pallas import tpu as pltpu
from jax.sharding import PartitionSpec as P

CHEB = 16

MESH = pl.DeviceIdType.MESH

time_step = 8.0


def ring(x, axis, step):
    count = lax.axis_size(axis)
    return lax.ppermute(x, axis, [(i, (i + step) % count) for i in range(count)])


def halos(cells):
    nd = cells.ndim
    dx, dy, dz = nd - 3, nd - 2, nd - 1
    x_lo = ring(lax.slice_in_dim(cells, cells.shape[dx] - 1, cells.shape[dx], axis=dx), "gx", 1)
    x_hi = ring(lax.slice_in_dim(cells, 0, 1, axis=dx), "gx", -1)
    y_lo = ring(lax.slice_in_dim(cells, cells.shape[dy] - 1, cells.shape[dy], axis=dy), "gy", 1)
    y_hi = ring(lax.slice_in_dim(cells, 0, 1, axis=dy), "gy", -1)
    ends = jnp.concatenate(
        [lax.slice_in_dim(cells, 0, 1, axis=dz), lax.slice_in_dim(cells, cells.shape[dz] - 1, cells.shape[dz], axis=dz)],
        axis=dz,
    )
    got = ring(ends, "pa", 1)
    z_lo = lax.slice_in_dim(got, 1, 2, axis=dz)
    z_hi = lax.slice_in_dim(got, 0, 1, axis=dz)
    return (x_lo, x_hi, y_lo, y_hi, z_lo, z_hi)


def neighbours(cells, faces):
    nd = cells.ndim
    out = []
    for k, dim in enumerate((nd - 3, nd - 2, nd - 1)):
        lo, hi = faces[2 * k], faces[2 * k + 1]
        n = cells.shape[dim]
        out.append(jnp.concatenate([lo, lax.slice_in_dim(cells, 0, n - 1, axis=dim)], axis=dim))
        out.append(jnp.concatenate([lax.slice_in_dim(cells, 1, n, axis=dim), hi], axis=dim))
    return out


def solve_kernel(ngx, ngy, ab_ref, w_ref, rhs_ref, d0_ref, x_ref, r_ref,
                 dbuf, sx, sy, sz, rx, ry, rz, send_sem, recv_sem):
    S, X, Y, Z = rhs_ref.shape
    gx = lax.axis_index("gx")
    gy = lax.axis_index("gy")
    pa = lax.axis_index("pa")
    gx_prev = lax.rem(gx + ngx - 1, ngx)
    gx_next = lax.rem(gx + 1, ngx)
    gy_prev = lax.rem(gy + ngy - 1, ngy)
    gy_next = lax.rem(gy + 1, ngy)
    partner = 1 - pa
    peers = ((gx_prev, gy, pa), (gx_next, gy, pa), (gx, gy_prev, pa), (gx, gy_next, pa), (gx, gy, partner))

    barrier = pltpu.get_barrier_semaphore()
    for dev in peers:
        pl.semaphore_signal(barrier, inc=1, device_id=dev, device_id_type=MESH)
    pl.semaphore_wait(barrier, len(peers))

    def copies(slot):
        plan = (
            (sx.at[0], rx.at[slot, 1], peers[0]),
            (sx.at[1], rx.at[slot, 0], peers[1]),
            (sy.at[0], ry.at[slot, 1], peers[2]),
            (sy.at[1], ry.at[slot, 0], peers[3]),
            (sz, rz.at[slot], peers[4]),
        )
        return [
            pltpu.make_async_remote_copy(
                src_ref=src, dst_ref=dst, send_sem=send_sem.at[i, slot], recv_sem=recv_sem.at[i, slot],
                device_id=dev, device_id_type=MESH,
            )
            for i, (src, dst, dev) in enumerate(plan)
        ]

    def put_faces(s, xi, plane):
        if xi == 0:
            sx[0, s] = plane
        if xi == X - 1:
            sx[1, s] = plane
        sy[0, s, pl.ds(xi, 1), :] = plane[0:1, :]
        sy[1, s, pl.ds(xi, 1), :] = plane[Y - 1:Y, :]
        t = plane.T
        sz[0, s, pl.ds(xi, 1), :] = t[0:1, :]
        sz[1, s, pl.ds(xi, 1), :] = t[Z - 1:Z, :]

    row = lax.broadcasted_iota(jnp.int32, (Y, Z), 0)
    lane = lax.broadcasted_iota(jnp.int32, (Y, Z), 1)

    for s in range(S):
        for xi in range(X):
            plane = d0_ref[s, xi]
            dbuf[0, s, xi] = plane
            x_ref[s, xi] = jnp.zeros((Y, Z), jnp.float32)
            r_ref[s, xi] = rhs_ref[s, xi]
            put_faces(s, xi, plane)
    for c in copies(0):
        c.start()

    def step(k, carry):
        slot = lax.rem(k, 2)
        nslot = 1 - slot
        for c in copies(slot):
            c.wait()
        a = ab_ref[0, k]
        b = ab_ref[1, k]
        last = k == CHEB - 1
        for s in range(S):
            for xi in range(X):
                c = dbuf[slot, s, xi]
                xm = dbuf[slot, s, xi - 1] if xi > 0 else rx[slot, 0, s]
                xp = dbuf[slot, s, xi + 1] if xi < X - 1 else rx[slot, 1, s]
                ym = jnp.where(row == 0, jnp.broadcast_to(ry[slot, 0, s, pl.ds(xi, 1), :], (Y, Z)),
                               pltpu.roll(c, 1, 0))
                yp = jnp.where(row == Y - 1, jnp.broadcast_to(ry[slot, 1, s, pl.ds(xi, 1), :], (Y, Z)),
                               pltpu.roll(c, Y - 1, 0))
                zpair = jnp.where(
                    row < Y // 2,
                    jnp.broadcast_to(rz[slot, 1, s, pl.ds(xi, 1), :], (Y, Z)),
                    jnp.broadcast_to(rz[slot, 0, s, pl.ds(xi, 1), :], (Y, Z)),
                ).T
                zm = jnp.where(lane == 0, zpair, pltpu.roll(c, 1, 1))
                zp = jnp.where(lane == Z - 1, zpair, pltpu.roll(c, Z - 1, 1))
                summed = w_ref[0, xi] * (c - xm)
                summed = summed + w_ref[1, xi] * (c - xp)
                summed = summed + w_ref[2, xi] * (c - ym)
                summed = summed + w_ref[3, xi] * (c - yp)
                summed = summed + w_ref[4, xi] * (c - zm)
                summed = summed + w_ref[5, xi] * (c - zp)
                x_ref[s, xi] = x_ref[s, xi] + c
                res = r_ref[s, xi] - (c + summed)
                r_ref[s, xi] = res
                nd = a * c + b * res
                dbuf[nslot, s, xi] = nd
                put_faces(s, xi, nd)

        @pl.when(jnp.logical_not(last))
        def _():
            for c in copies(nslot):
                c.start()

        return carry

    lax.fori_loop(0, CHEB, step, 0)


def chebyshev_solve(weights, rhs, d0, ab):
    S, X, Y, Z = rhs.shape
    ngx = lax.axis_size("gx")
    ngy = lax.axis_size("gy")
    f32 = jnp.float32
    vmem = pl.BlockSpec(memory_space=pltpu.VMEM)
    return pl.pallas_call(
        functools.partial(solve_kernel, ngx, ngy),
        out_shape=(jax.ShapeDtypeStruct(rhs.shape, f32), jax.ShapeDtypeStruct(rhs.shape, f32)),
        in_specs=[pl.BlockSpec(memory_space=pltpu.SMEM), vmem, vmem, vmem],
        out_specs=(vmem, vmem),
        scratch_shapes=[
            pltpu.VMEM((2, S, X, Y, Z), f32),
            pltpu.VMEM((2, S, Y, Z), f32),
            pltpu.VMEM((2, S, X, Z), f32),
            pltpu.VMEM((2, S, X, Y), f32),
            pltpu.VMEM((2, 2, S, Y, Z), f32),
            pltpu.VMEM((2, 2, S, X, Z), f32),
            pltpu.VMEM((2, 2, S, X, Y), f32),
            pltpu.SemaphoreType.DMA((5, 2)),
            pltpu.SemaphoreType.DMA((5, 2)),
        ],
        compiler_params=pltpu.CompilerParams(
            collective_id=0, has_side_effects=True, vmem_limit_bytes=60 * 1024 * 1024
        ),
    )(ab, weights, rhs, d0)


def body(conductivity, stored_state, row_scales, cotangent, upper_bound):
    upper = upper_bound[0]
    weights = jnp.stack([(conductivity + kn) * (0.5 * time_step) for kn in neighbours(conductivity, halos(conductivity))])
    partner = ring(stored_state, "pa", 1)
    previous = partner.astype(jnp.float32) * row_scales[:, :, None]
    rhs = jnp.stack((previous, cotangent))

    theta = 0.5 * (upper + 1.0)
    delta = 0.5 * (upper - 1.0)
    sigma = theta / delta
    rho = 1.0 / sigma
    coefs = []
    for _ in range(CHEB):
        rho_next = 1.0 / (2.0 * sigma - rho)
        coefs.append((rho_next * rho, 2.0 * rho_next / delta))
        rho = rho_next
    ab = jnp.stack([jnp.stack([c[0] for c in coefs]), jnp.stack([c[1] for c in coefs])])

    solved, residuals = chebyshev_solve(weights, rhs, rhs / theta, ab)
    near = neighbours(solved, halos(solved))
    summed = jnp.zeros_like(solved[0])
    for n in near:
        differ = solved - n
        summed = summed + differ[0] * differ[1]
    grad_conductivity = -0.5 * time_step * summed
    return (grad_conductivity, solved[1], solved[0], residuals)


def solution(mesh):
    return jax.shard_map(
        body,
        mesh=mesh,
        in_specs=(
            P("gx", "gy", "pa"),
            P("gx", "gy", "pa"),
            P("gx", "gy"),
            P("gx", "gy", "pa"),
            P(),
        ),
        out_specs=(
            P("gx", "gy", "pa"),
            P("gx", "gy", "pa"),
            P("gx", "gy", "pa"),
            P(None, "gx", "gy", "pa"),
        ),
        check_vma=False,
    )
```

```python
import functools

import jax
import jax.numpy as jnp
from jax import lax
from jax.experimental import pallas as pl
from jax.experimental.pallas import tpu as pltpu
from jax.sharding import PartitionSpec as P

CHEB = 16

MESH = pl.DeviceIdType.MESH

time_step = 8.0


def ring(x, axis, step):
    count = lax.axis_size(axis)
    return lax.ppermute(x, axis, [(i, (i + step) % count) for i in range(count)])


def halos(cells):
    nd = cells.ndim
    dx, dy, dz = nd - 3, nd - 2, nd - 1
    x_lo = ring(lax.slice_in_dim(cells, cells.shape[dx] - 1, cells.shape[dx], axis=dx), "gx", 1)
    x_hi = ring(lax.slice_in_dim(cells, 0, 1, axis=dx), "gx", -1)
    y_lo = ring(lax.slice_in_dim(cells, cells.shape[dy] - 1, cells.shape[dy], axis=dy), "gy", 1)
    y_hi = ring(lax.slice_in_dim(cells, 0, 1, axis=dy), "gy", -1)
    ends = jnp.concatenate(
        [lax.slice_in_dim(cells, 0, 1, axis=dz), lax.slice_in_dim(cells, cells.shape[dz] - 1, cells.shape[dz], axis=dz)],
        axis=dz,
    )
    got = ring(ends, "pa", 1)
    z_lo = lax.slice_in_dim(got, 1, 2, axis=dz)
    z_hi = lax.slice_in_dim(got, 0, 1, axis=dz)
    return (x_lo, x_hi, y_lo, y_hi, z_lo, z_hi)


def neighbours(cells, faces):
    nd = cells.ndim
    out = []
    for k, dim in enumerate((nd - 3, nd - 2, nd - 1)):
        lo, hi = faces[2 * k], faces[2 * k + 1]
        n = cells.shape[dim]
        out.append(jnp.concatenate([lo, lax.slice_in_dim(cells, 0, n - 1, axis=dim)], axis=dim))
        out.append(jnp.concatenate([lax.slice_in_dim(cells, 1, n, axis=dim), hi], axis=dim))
    return out


def solve_kernel(ngx, ngy, ab_ref, w_ref, rhs_ref, d0_ref, g_ref, adj_ref, state_ref, r_ref,
                 dbuf, sx, sy, sz, rx, ry, rz, send_sem, recv_sem):
    S, X, Y, Z = rhs_ref.shape
    xo = (state_ref, adj_ref)
    gx = lax.axis_index("gx")
    gy = lax.axis_index("gy")
    pa = lax.axis_index("pa")
    gx_prev = lax.rem(gx + ngx - 1, ngx)
    gx_next = lax.rem(gx + 1, ngx)
    gy_prev = lax.rem(gy + ngy - 1, ngy)
    gy_next = lax.rem(gy + 1, ngy)
    partner = 1 - pa
    peers = ((gx_prev, gy, pa), (gx_next, gy, pa), (gx, gy_prev, pa), (gx, gy_next, pa), (gx, gy, partner))

    barrier = pltpu.get_barrier_semaphore()
    for dev in peers:
        pl.semaphore_signal(barrier, inc=1, device_id=dev, device_id_type=MESH)
    pl.semaphore_wait(barrier, len(peers))

    def copies(slot):
        plan = (
            (sx.at[0], rx.at[slot, 1], peers[0]),
            (sx.at[1], rx.at[slot, 0], peers[1]),
            (sy.at[0], ry.at[slot, 1], peers[2]),
            (sy.at[1], ry.at[slot, 0], peers[3]),
            (sz, rz.at[slot], peers[4]),
        )
        return [
            pltpu.make_async_remote_copy(
                src_ref=src, dst_ref=dst, send_sem=send_sem.at[i, slot], recv_sem=recv_sem.at[i, slot],
                device_id=dev, device_id_type=MESH,
            )
            for i, (src, dst, dev) in enumerate(plan)
        ]

    def put_faces(s, xi, plane):
        if xi == 0:
            sx[0, s] = plane
        if xi == X - 1:
            sx[1, s] = plane
        sy[0, s, pl.ds(xi, 1), :] = plane[0:1, :]
        sy[1, s, pl.ds(xi, 1), :] = plane[Y - 1:Y, :]
        t = plane.T
        sz[0, s, pl.ds(xi, 1), :] = t[0:1, :]
        sz[1, s, pl.ds(xi, 1), :] = t[Z - 1:Z, :]

    row = lax.broadcasted_iota(jnp.int32, (Y, Z), 0)
    lane = lax.broadcasted_iota(jnp.int32, (Y, Z), 1)

    def near(plane, slot, s, xi):
        c = plane(xi)
        xm = plane(xi - 1) if xi > 0 else rx[slot, 0, s]
        xp = plane(xi + 1) if xi < X - 1 else rx[slot, 1, s]
        ym = jnp.where(row == 0, jnp.broadcast_to(ry[slot, 0, s, pl.ds(xi, 1), :], (Y, Z)), pltpu.roll(c, 1, 0))
        yp = jnp.where(row == Y - 1, jnp.broadcast_to(ry[slot, 1, s, pl.ds(xi, 1), :], (Y, Z)),
                       pltpu.roll(c, Y - 1, 0))
        zpair = jnp.where(
            row < Y // 2,
            jnp.broadcast_to(rz[slot, 1, s, pl.ds(xi, 1), :], (Y, Z)),
            jnp.broadcast_to(rz[slot, 0, s, pl.ds(xi, 1), :], (Y, Z)),
        ).T
        zm = jnp.where(lane == 0, zpair, pltpu.roll(c, 1, 1))
        zp = jnp.where(lane == Z - 1, zpair, pltpu.roll(c, Z - 1, 1))
        return c, (xm, xp, ym, yp, zm, zp)

    for s in range(S):
        for xi in range(X):
            plane = d0_ref[s, xi]
            dbuf[0, s, xi] = plane
            xo[s][xi] = jnp.zeros((Y, Z), jnp.float32)
            r_ref[s, xi] = rhs_ref[s, xi]
            put_faces(s, xi, plane)
    for c in copies(0):
        c.start()

    def step(k, slot, final):
        nslot = 1 - slot
        for c in copies(slot):
            c.wait()
        a = ab_ref[0, k]
        b = ab_ref[1, k]
        for s in range(S):
            for xi in range(X):
                c, nb = near(lambda i: dbuf[slot, s, i], slot, s, xi)
                summed = w_ref[0, xi] * (c - nb[0])
                for j in range(1, 6):
                    summed = summed + w_ref[j, xi] * (c - nb[j])
                xn = xo[s][xi] + c
                xo[s][xi] = xn
                res = r_ref[s, xi] - (c + summed)
                r_ref[s, xi] = res
                if final:
                    put_faces(s, xi, xn)
                else:
                    nd = a * c + b * res
                    dbuf[nslot, s, xi] = nd
                    put_faces(s, xi, nd)
        for c in copies(nslot):
            c.start()

    def loop_step(k, carry):
        step(k, lax.rem(k, 2), False)
        return carry

    lax.fori_loop(0, CHEB - 1, loop_step, 0)
    step(CHEB - 1, (CHEB - 1) % 2, True)

    gslot = CHEB % 2
    for c in copies(gslot):
        c.wait()
    for xi in range(X):
        c0, n0 = near(lambda i: xo[0][i], gslot, 0, xi)
        c1, n1 = near(lambda i: xo[1][i], gslot, 1, xi)
        summed = (c0 - n0[0]) * (c1 - n1[0])
        for j in range(1, 6):
            summed = summed + (c0 - n0[j]) * (c1 - n1[j])
        g_ref[xi] = (-0.5 * time_step) * summed


def chebyshev_solve(weights, rhs, d0, ab):
    S, X, Y, Z = rhs.shape
    ngx = lax.axis_size("gx")
    ngy = lax.axis_size("gy")
    f32 = jnp.float32
    vmem = pl.BlockSpec(memory_space=pltpu.VMEM)
    field = jax.ShapeDtypeStruct((X, Y, Z), f32)
    return pl.pallas_call(
        functools.partial(solve_kernel, ngx, ngy),
        out_shape=(field, field, field, jax.ShapeDtypeStruct(rhs.shape, f32)),
        in_specs=[pl.BlockSpec(memory_space=pltpu.SMEM), vmem, vmem, vmem],
        out_specs=(vmem, vmem, vmem, vmem),
        scratch_shapes=[
            pltpu.VMEM((2, S, X, Y, Z), f32),
            pltpu.VMEM((2, S, Y, Z), f32),
            pltpu.VMEM((2, S, X, Z), f32),
            pltpu.VMEM((2, S, X, Y), f32),
            pltpu.VMEM((2, 2, S, Y, Z), f32),
            pltpu.VMEM((2, 2, S, X, Z), f32),
            pltpu.VMEM((2, 2, S, X, Y), f32),
            pltpu.SemaphoreType.DMA((5, 2)),
            pltpu.SemaphoreType.DMA((5, 2)),
        ],
        compiler_params=pltpu.CompilerParams(
            collective_id=0, has_side_effects=True, vmem_limit_bytes=60 * 1024 * 1024
        ),
    )(ab, weights, rhs, d0)


def body(conductivity, stored_state, row_scales, cotangent, upper_bound):
    upper = upper_bound[0]
    weights = jnp.stack([(conductivity + kn) * (0.5 * time_step) for kn in neighbours(conductivity, halos(conductivity))])
    partner = ring(stored_state, "pa", 1)
    previous = partner.astype(jnp.float32) * row_scales[:, :, None]
    rhs = jnp.stack((previous, cotangent))

    theta = 0.5 * (upper + 1.0)
    delta = 0.5 * (upper - 1.0)
    sigma = theta / delta
    rho = 1.0 / sigma
    coefs = []
    for _ in range(CHEB):
        rho_next = 1.0 / (2.0 * sigma - rho)
        coefs.append((rho_next * rho, 2.0 * rho_next / delta))
        rho = rho_next
    ab = jnp.stack([jnp.stack([c[0] for c in coefs]), jnp.stack([c[1] for c in coefs])])

    return chebyshev_solve(weights, rhs, rhs / theta, ab)


def solution(mesh):
    return jax.shard_map(
        body,
        mesh=mesh,
        in_specs=(
            P("gx", "gy", "pa"),
            P("gx", "gy", "pa"),
            P("gx", "gy"),
            P("gx", "gy", "pa"),
            P(),
        ),
        out_specs=(
            P("gx", "gy", "pa"),
            P("gx", "gy", "pa"),
            P("gx", "gy", "pa"),
            P(None, "gx", "gy", "pa"),
        ),
        check_vma=False,
    )
```

```python
import functools

import jax
import jax.numpy as jnp
from jax import lax
from jax.experimental import pallas as pl
from jax.experimental.pallas import tpu as pltpu
from jax.sharding import PartitionSpec as P

CHEB = 16

MESH = pl.DeviceIdType.MESH

time_step = 8.0


def ring(x, axis, step):
    count = lax.axis_size(axis)
    return lax.ppermute(x, axis, [(i, (i + step) % count) for i in range(count)])


def halos(cells):
    nd = cells.ndim
    dx, dy, dz = nd - 3, nd - 2, nd - 1
    x_lo = ring(lax.slice_in_dim(cells, cells.shape[dx] - 1, cells.shape[dx], axis=dx), "gx", 1)
    x_hi = ring(lax.slice_in_dim(cells, 0, 1, axis=dx), "gx", -1)
    y_lo = ring(lax.slice_in_dim(cells, cells.shape[dy] - 1, cells.shape[dy], axis=dy), "gy", 1)
    y_hi = ring(lax.slice_in_dim(cells, 0, 1, axis=dy), "gy", -1)
    ends = jnp.concatenate(
        [lax.slice_in_dim(cells, 0, 1, axis=dz), lax.slice_in_dim(cells, cells.shape[dz] - 1, cells.shape[dz], axis=dz)],
        axis=dz,
    )
    got = ring(ends, "pa", 1)
    z_lo = lax.slice_in_dim(got, 1, 2, axis=dz)
    z_hi = lax.slice_in_dim(got, 0, 1, axis=dz)
    return (x_lo, x_hi, y_lo, y_hi, z_lo, z_hi)


def neighbours(cells, faces):
    nd = cells.ndim
    out = []
    for k, dim in enumerate((nd - 3, nd - 2, nd - 1)):
        lo, hi = faces[2 * k], faces[2 * k + 1]
        n = cells.shape[dim]
        out.append(jnp.concatenate([lo, lax.slice_in_dim(cells, 0, n - 1, axis=dim)], axis=dim))
        out.append(jnp.concatenate([lax.slice_in_dim(cells, 1, n, axis=dim), hi], axis=dim))
    return out


def solve_kernel(ngx, ngy, ab_ref, w_ref, rhs_ref, d0_ref, g_ref, adj_ref, state_ref, r_ref,
                 dbuf, sx, sy, sz, rx, ry, rz, send_sem, recv_sem):
    S, X, Y, Z = rhs_ref.shape
    xo = (state_ref, adj_ref)
    gx = lax.axis_index("gx")
    gy = lax.axis_index("gy")
    pa = lax.axis_index("pa")
    gx_prev = lax.rem(gx + ngx - 1, ngx)
    gx_next = lax.rem(gx + 1, ngx)
    gy_prev = lax.rem(gy + ngy - 1, ngy)
    gy_next = lax.rem(gy + 1, ngy)
    partner = 1 - pa
    peers = ((gx_prev, gy, pa), (gx_next, gy, pa), (gx, gy_prev, pa), (gx, gy_next, pa), (gx, gy, partner))

    barrier = pltpu.get_barrier_semaphore()
    for dev in peers:
        pl.semaphore_signal(barrier, inc=1, device_id=dev, device_id_type=MESH)
    pl.semaphore_wait(barrier, len(peers))

    def copies(slot):
        plan = (
            (sx.at[0], rx.at[slot, 1], peers[0]),
            (sx.at[1], rx.at[slot, 0], peers[1]),
            (sy.at[0], ry.at[slot, 1], peers[2]),
            (sy.at[1], ry.at[slot, 0], peers[3]),
            (sz, rz.at[slot], peers[4]),
        )
        return [
            pltpu.make_async_remote_copy(
                src_ref=src, dst_ref=dst, send_sem=send_sem.at[i, slot], recv_sem=recv_sem.at[i, slot],
                device_id=dev, device_id_type=MESH,
            )
            for i, (src, dst, dev) in enumerate(plan)
        ]

    def put_faces(s, xi, plane):
        if xi == 0:
            sx[0, s] = plane
        if xi == X - 1:
            sx[1, s] = plane
        sy[0, s, pl.ds(xi, 1), :] = plane[0:1, :]
        sy[1, s, pl.ds(xi, 1), :] = plane[Y - 1:Y, :]
        t = plane.T
        sz[0, s, pl.ds(xi, 1), :] = t[0:1, :]
        sz[1, s, pl.ds(xi, 1), :] = t[Z - 1:Z, :]

    row = lax.broadcasted_iota(jnp.int32, (Y, Z), 0)
    lane = lax.broadcasted_iota(jnp.int32, (Y, Z), 1)

    def near(plane, slot, s, xi):
        c = plane(xi)
        xm = plane(xi - 1) if xi > 0 else rx[slot, 0, s]
        xp = plane(xi + 1) if xi < X - 1 else rx[slot, 1, s]
        ym = jnp.where(row == 0, jnp.broadcast_to(ry[slot, 0, s, pl.ds(xi, 1), :], (Y, Z)), pltpu.roll(c, 1, 0))
        yp = jnp.where(row == Y - 1, jnp.broadcast_to(ry[slot, 1, s, pl.ds(xi, 1), :], (Y, Z)),
                       pltpu.roll(c, Y - 1, 0))
        zpair = jnp.where(
            row < Y // 2,
            jnp.broadcast_to(rz[slot, 1, s, pl.ds(xi, 1), :], (Y, Z)),
            jnp.broadcast_to(rz[slot, 0, s, pl.ds(xi, 1), :], (Y, Z)),
        ).T
        zm = jnp.where(lane == 0, zpair, pltpu.roll(c, 1, 1))
        zp = jnp.where(lane == Z - 1, zpair, pltpu.roll(c, Z - 1, 1))
        return c, (xm, xp, ym, yp, zm, zp)

    for s in range(S):
        for xi in range(X):
            plane = d0_ref[s, xi]
            dbuf[0, s, xi] = plane
            xo[s][xi] = jnp.zeros((Y, Z), jnp.float32)
            r_ref[s, xi] = rhs_ref[s, xi]
            put_faces(s, xi, plane)
    for c in copies(0):
        c.start()

    def step(k, slot, final):
        nslot = 1 - slot
        for c in copies(slot):
            c.wait()
        a = ab_ref[0, k]
        b = ab_ref[1, k]
        outgoing = copies(nslot)
        order = [(s, xi) for xi in (0, X - 1) for s in range(S)] + [(s, xi) for xi in range(1, X - 1) for s in range(S)]
        for n, (s, xi) in enumerate(order):
            if n == 2 * S:
                for c in outgoing[:2]:
                    c.start()
            c, nb = near(lambda i: dbuf[slot, s, i], slot, s, xi)
            summed = w_ref[0, xi] * (c - nb[0])
            for j in range(1, 6):
                summed = summed + w_ref[j, xi] * (c - nb[j])
            xn = xo[s][xi] + c
            xo[s][xi] = xn
            res = r_ref[s, xi] - (c + summed)
            r_ref[s, xi] = res
            if final:
                put_faces(s, xi, xn)
            else:
                nd = a * c + b * res
                dbuf[nslot, s, xi] = nd
                put_faces(s, xi, nd)
        for c in outgoing[2:]:
            c.start()

    def loop_step(k, carry):
        step(k, lax.rem(k, 2), False)
        return carry

    lax.fori_loop(0, CHEB - 1, loop_step, 0)
    step(CHEB - 1, (CHEB - 1) % 2, True)

    gslot = CHEB % 2
    for c in copies(gslot):
        c.wait()
    for xi in range(X):
        c0, n0 = near(lambda i: xo[0][i], gslot, 0, xi)
        c1, n1 = near(lambda i: xo[1][i], gslot, 1, xi)
        summed = (c0 - n0[0]) * (c1 - n1[0])
        for j in range(1, 6):
            summed = summed + (c0 - n0[j]) * (c1 - n1[j])
        g_ref[xi] = (-0.5 * time_step) * summed


def chebyshev_solve(weights, rhs, d0, ab):
    S, X, Y, Z = rhs.shape
    ngx = lax.axis_size("gx")
    ngy = lax.axis_size("gy")
    f32 = jnp.float32
    vmem = pl.BlockSpec(memory_space=pltpu.VMEM)
    field = jax.ShapeDtypeStruct((X, Y, Z), f32)
    return pl.pallas_call(
        functools.partial(solve_kernel, ngx, ngy),
        out_shape=(field, field, field, jax.ShapeDtypeStruct(rhs.shape, f32)),
        in_specs=[pl.BlockSpec(memory_space=pltpu.SMEM), vmem, vmem, vmem],
        out_specs=(vmem, vmem, vmem, vmem),
        scratch_shapes=[
            pltpu.VMEM((2, S, X, Y, Z), f32),
            pltpu.VMEM((2, S, Y, Z), f32),
            pltpu.VMEM((2, S, X, Z), f32),
            pltpu.VMEM((2, S, X, Y), f32),
            pltpu.VMEM((2, 2, S, Y, Z), f32),
            pltpu.VMEM((2, 2, S, X, Z), f32),
            pltpu.VMEM((2, 2, S, X, Y), f32),
            pltpu.SemaphoreType.DMA((5, 2)),
            pltpu.SemaphoreType.DMA((5, 2)),
        ],
        compiler_params=pltpu.CompilerParams(
            collective_id=0, has_side_effects=True, vmem_limit_bytes=60 * 1024 * 1024
        ),
    )(ab, weights, rhs, d0)


def body(conductivity, stored_state, row_scales, cotangent, upper_bound):
    upper = upper_bound[0]
    weights = jnp.stack([(conductivity + kn) * (0.5 * time_step) for kn in neighbours(conductivity, halos(conductivity))])
    partner = ring(stored_state, "pa", 1)
    previous = partner.astype(jnp.float32) * row_scales[:, :, None]
    rhs = jnp.stack((previous, cotangent))

    theta = 0.5 * (upper + 1.0)
    delta = 0.5 * (upper - 1.0)
    sigma = theta / delta
    rho = 1.0 / sigma
    coefs = []
    for _ in range(CHEB):
        rho_next = 1.0 / (2.0 * sigma - rho)
        coefs.append((rho_next * rho, 2.0 * rho_next / delta))
        rho = rho_next
    ab = jnp.stack([jnp.stack([c[0] for c in coefs]), jnp.stack([c[1] for c in coefs])])

    return chebyshev_solve(weights, rhs, rhs / theta, ab)


def solution(mesh):
    return jax.shard_map(
        body,
        mesh=mesh,
        in_specs=(
            P("gx", "gy", "pa"),
            P("gx", "gy", "pa"),
            P("gx", "gy"),
            P("gx", "gy", "pa"),
            P(),
        ),
        out_specs=(
            P("gx", "gy", "pa"),
            P("gx", "gy", "pa"),
            P("gx", "gy", "pa"),
            P(None, "gx", "gy", "pa"),
        ),
        check_vma=False,
    )
```

```python
import functools

import jax
import jax.numpy as jnp
from jax import lax
from jax.experimental import pallas as pl
from jax.experimental.pallas import tpu as pltpu
from jax.sharding import PartitionSpec as P

CHEB = 16

MESH = pl.DeviceIdType.MESH

time_step = 8.0


def ring(x, axis, step):
    count = lax.axis_size(axis)
    return lax.ppermute(x, axis, [(i, (i + step) % count) for i in range(count)])


def halos(cells):
    nd = cells.ndim
    dx, dy, dz = nd - 3, nd - 2, nd - 1
    x_lo = ring(lax.slice_in_dim(cells, cells.shape[dx] - 1, cells.shape[dx], axis=dx), "gx", 1)
    x_hi = ring(lax.slice_in_dim(cells, 0, 1, axis=dx), "gx", -1)
    y_lo = ring(lax.slice_in_dim(cells, cells.shape[dy] - 1, cells.shape[dy], axis=dy), "gy", 1)
    y_hi = ring(lax.slice_in_dim(cells, 0, 1, axis=dy), "gy", -1)
    ends = jnp.concatenate(
        [lax.slice_in_dim(cells, 0, 1, axis=dz), lax.slice_in_dim(cells, cells.shape[dz] - 1, cells.shape[dz], axis=dz)],
        axis=dz,
    )
    got = ring(ends, "pa", 1)
    z_lo = lax.slice_in_dim(got, 1, 2, axis=dz)
    z_hi = lax.slice_in_dim(got, 0, 1, axis=dz)
    return (x_lo, x_hi, y_lo, y_hi, z_lo, z_hi)


def neighbours(cells, faces):
    nd = cells.ndim
    out = []
    for k, dim in enumerate((nd - 3, nd - 2, nd - 1)):
        lo, hi = faces[2 * k], faces[2 * k + 1]
        n = cells.shape[dim]
        out.append(jnp.concatenate([lo, lax.slice_in_dim(cells, 0, n - 1, axis=dim)], axis=dim))
        out.append(jnp.concatenate([lax.slice_in_dim(cells, 1, n, axis=dim), hi], axis=dim))
    return out


def solve_kernel(ngx, ngy, ab_ref, w_ref, rhs_ref, d0_ref, g_ref, adj_ref, state_ref, r_ref,
                 dbuf, sx, sy, sz, rx, ry, rz, send_sem, recv_sem):
    S, X, Y, Z = rhs_ref.shape
    xo = (state_ref, adj_ref)
    gx = lax.axis_index("gx")
    gy = lax.axis_index("gy")
    pa = lax.axis_index("pa")
    gx_prev = lax.rem(gx + ngx - 1, ngx)
    gx_next = lax.rem(gx + 1, ngx)
    gy_prev = lax.rem(gy + ngy - 1, ngy)
    gy_next = lax.rem(gy + 1, ngy)
    partner = 1 - pa
    peers = ((gx_prev, gy, pa), (gx_next, gy, pa), (gx, gy_prev, pa), (gx, gy_next, pa), (gx, gy, partner))

    barrier = pltpu.get_barrier_semaphore()
    for dev in peers:
        pl.semaphore_signal(barrier, inc=1, device_id=dev, device_id_type=MESH)
    pl.semaphore_wait(barrier, len(peers))

    def copies(slot, s):
        plan = (
            (sx.at[0, s], rx.at[slot, 1, s], peers[0]),
            (sx.at[1, s], rx.at[slot, 0, s], peers[1]),
            (sy.at[0, s], ry.at[slot, 1, s], peers[2]),
            (sy.at[1, s], ry.at[slot, 0, s], peers[3]),
            (sz.at[s], rz.at[slot, s], peers[4]),
        )
        return [
            pltpu.make_async_remote_copy(
                src_ref=src, dst_ref=dst, send_sem=send_sem.at[i, s, slot], recv_sem=recv_sem.at[i, s, slot],
                device_id=dev, device_id_type=MESH,
            )
            for i, (src, dst, dev) in enumerate(plan)
        ]

    def put_faces(s, xi, plane):
        if xi == 0:
            sx[0, s] = plane
        if xi == X - 1:
            sx[1, s] = plane
        sy[0, s, pl.ds(xi, 1), :] = plane[0:1, :]
        sy[1, s, pl.ds(xi, 1), :] = plane[Y - 1:Y, :]
        t = plane.T
        sz[s, 0, pl.ds(xi, 1), :] = t[0:1, :]
        sz[s, 1, pl.ds(xi, 1), :] = t[Z - 1:Z, :]

    row = lax.broadcasted_iota(jnp.int32, (Y, Z), 0)
    lane = lax.broadcasted_iota(jnp.int32, (Y, Z), 1)

    def near(plane, slot, s, xi):
        c = plane(xi)
        xm = plane(xi - 1) if xi > 0 else rx[slot, 0, s]
        xp = plane(xi + 1) if xi < X - 1 else rx[slot, 1, s]
        ym = jnp.where(row == 0, jnp.broadcast_to(ry[slot, 0, s, pl.ds(xi, 1), :], (Y, Z)), pltpu.roll(c, 1, 0))
        yp = jnp.where(row == Y - 1, jnp.broadcast_to(ry[slot, 1, s, pl.ds(xi, 1), :], (Y, Z)),
                       pltpu.roll(c, Y - 1, 0))
        zpair = jnp.where(
            row < Y // 2,
            jnp.broadcast_to(rz[slot, s, 1, pl.ds(xi, 1), :], (Y, Z)),
            jnp.broadcast_to(rz[slot, s, 0, pl.ds(xi, 1), :], (Y, Z)),
        ).T
        zm = jnp.where(lane == 0, zpair, pltpu.roll(c, 1, 1))
        zp = jnp.where(lane == Z - 1, zpair, pltpu.roll(c, Z - 1, 1))
        return c, (xm, xp, ym, yp, zm, zp)

    for s in range(S):
        for xi in range(X):
            plane = d0_ref[s, xi]
            dbuf[0, s, xi] = plane
            xo[s][xi] = jnp.zeros((Y, Z), jnp.float32)
            r_ref[s, xi] = rhs_ref[s, xi]
            put_faces(s, xi, plane)
        for c in copies(0, s):
            c.start()

    def step(k, slot, final):
        nslot = 1 - slot
        a = ab_ref[0, k]
        b = ab_ref[1, k]
        for s in range(S):
            for c in copies(slot, s):
                c.wait()
            outgoing = copies(nslot, s)
            for xi in [0, X - 1] + list(range(1, X - 1)):
                if xi == 1:
                    for c in outgoing[:2]:
                        c.start()
                c, nb = near(lambda i: dbuf[slot, s, i], slot, s, xi)
                summed = w_ref[0, xi] * (c - nb[0])
                for j in range(1, 6):
                    summed = summed + w_ref[j, xi] * (c - nb[j])
                xn = xo[s][xi] + c
                xo[s][xi] = xn
                res = r_ref[s, xi] - (c + summed)
                r_ref[s, xi] = res
                if final:
                    put_faces(s, xi, xn)
                else:
                    nd = a * c + b * res
                    dbuf[nslot, s, xi] = nd
                    put_faces(s, xi, nd)
            for c in outgoing[2:]:
                c.start()

    def loop_step(k, carry):
        step(k, lax.rem(k, 2), False)
        return carry

    lax.fori_loop(0, CHEB - 1, loop_step, 0)
    step(CHEB - 1, (CHEB - 1) % 2, True)

    gslot = CHEB % 2
    for s in range(S):
        for c in copies(gslot, s):
            c.wait()
    for xi in range(X):
        c0, n0 = near(lambda i: xo[0][i], gslot, 0, xi)
        c1, n1 = near(lambda i: xo[1][i], gslot, 1, xi)
        summed = (c0 - n0[0]) * (c1 - n1[0])
        for j in range(1, 6):
            summed = summed + (c0 - n0[j]) * (c1 - n1[j])
        g_ref[xi] = (-0.5 * time_step) * summed


def chebyshev_solve(weights, rhs, d0, ab):
    S, X, Y, Z = rhs.shape
    ngx = lax.axis_size("gx")
    ngy = lax.axis_size("gy")
    f32 = jnp.float32
    vmem = pl.BlockSpec(memory_space=pltpu.VMEM)
    field = jax.ShapeDtypeStruct((X, Y, Z), f32)
    return pl.pallas_call(
        functools.partial(solve_kernel, ngx, ngy),
        out_shape=(field, field, field, jax.ShapeDtypeStruct(rhs.shape, f32)),
        in_specs=[pl.BlockSpec(memory_space=pltpu.SMEM), vmem, vmem, vmem],
        out_specs=(vmem, vmem, vmem, vmem),
        scratch_shapes=[
            pltpu.VMEM((2, S, X, Y, Z), f32),
            pltpu.VMEM((2, S, Y, Z), f32),
            pltpu.VMEM((2, S, X, Z), f32),
            pltpu.VMEM((S, 2, X, Y), f32),
            pltpu.VMEM((2, 2, S, Y, Z), f32),
            pltpu.VMEM((2, 2, S, X, Z), f32),
            pltpu.VMEM((2, S, 2, X, Y), f32),
            pltpu.SemaphoreType.DMA((5, S, 2)),
            pltpu.SemaphoreType.DMA((5, S, 2)),
        ],
        compiler_params=pltpu.CompilerParams(
            collective_id=0, has_side_effects=True, vmem_limit_bytes=60 * 1024 * 1024
        ),
    )(ab, weights, rhs, d0)


def body(conductivity, stored_state, row_scales, cotangent, upper_bound):
    upper = upper_bound[0]
    weights = jnp.stack([(conductivity + kn) * (0.5 * time_step) for kn in neighbours(conductivity, halos(conductivity))])
    partner = ring(stored_state, "pa", 1)
    previous = partner.astype(jnp.float32) * row_scales[:, :, None]
    rhs = jnp.stack((previous, cotangent))

    theta = 0.5 * (upper + 1.0)
    delta = 0.5 * (upper - 1.0)
    sigma = theta / delta
    rho = 1.0 / sigma
    coefs = []
    for _ in range(CHEB):
        rho_next = 1.0 / (2.0 * sigma - rho)
        coefs.append((rho_next * rho, 2.0 * rho_next / delta))
        rho = rho_next
    ab = jnp.stack([jnp.stack([c[0] for c in coefs]), jnp.stack([c[1] for c in coefs])])

    return chebyshev_solve(weights, rhs, rhs / theta, ab)


def solution(mesh):
    return jax.shard_map(
        body,
        mesh=mesh,
        in_specs=(
            P("gx", "gy", "pa"),
            P("gx", "gy", "pa"),
            P("gx", "gy"),
            P("gx", "gy", "pa"),
            P(),
        ),
        out_specs=(
            P("gx", "gy", "pa"),
            P("gx", "gy", "pa"),
            P("gx", "gy", "pa"),
            P(None, "gx", "gy", "pa"),
        ),
        check_vma=False,
    )
```

```python
import functools

import jax
import jax.numpy as jnp
from jax import lax
from jax.experimental import pallas as pl
from jax.experimental.pallas import tpu as pltpu
from jax.sharding import PartitionSpec as P

CHEB = 16

MESH = pl.DeviceIdType.MESH

time_step = 8.0


def solve_kernel(ngx, ngy, ab_ref, kap_ref, st_ref, rs_ref, cot_ref, g_ref, adj_ref, state_ref, r_ref,
                 w_ref, prev, dbuf, sx, sy, sz, rx, ry, rz, send_sem, recv_sem, st_sem):
    S = 2
    X, Y, Z = kap_ref.shape
    xo = (state_ref, adj_ref)
    gx = lax.axis_index("gx")
    gy = lax.axis_index("gy")
    pa = lax.axis_index("pa")
    gx_prev = lax.rem(gx + ngx - 1, ngx)
    gx_next = lax.rem(gx + 1, ngx)
    gy_prev = lax.rem(gy + ngy - 1, ngy)
    gy_next = lax.rem(gy + 1, ngy)
    partner = 1 - pa
    peers = ((gx_prev, gy, pa), (gx_next, gy, pa), (gx, gy_prev, pa), (gx, gy_next, pa), (gx, gy, partner))

    barrier = pltpu.get_barrier_semaphore()
    for dev in peers:
        pl.semaphore_signal(barrier, inc=1, device_id=dev, device_id_type=MESH)
    pl.semaphore_wait(barrier, len(peers))

    def copies(slot, s):
        plan = (
            (sx.at[0, s], rx.at[slot, 1, s], peers[0]),
            (sx.at[1, s], rx.at[slot, 0, s], peers[1]),
            (sy.at[0, s], ry.at[slot, 1, s], peers[2]),
            (sy.at[1, s], ry.at[slot, 0, s], peers[3]),
            (sz.at[s], rz.at[slot, s], peers[4]),
        )
        return [
            pltpu.make_async_remote_copy(
                src_ref=src, dst_ref=dst, send_sem=send_sem.at[i, s, slot], recv_sem=recv_sem.at[i, s, slot],
                device_id=dev, device_id_type=MESH,
            )
            for i, (src, dst, dev) in enumerate(plan)
        ]

    def put_faces(s, xi, plane):
        if xi == 0:
            sx[0, s] = plane
        if xi == X - 1:
            sx[1, s] = plane
        sy[0, s, pl.ds(xi, 1), :] = plane[0:1, :]
        sy[1, s, pl.ds(xi, 1), :] = plane[Y - 1:Y, :]
        t = plane.T
        sz[s, 0, pl.ds(xi, 1), :] = t[0:1, :]
        sz[s, 1, pl.ds(xi, 1), :] = t[Z - 1:Z, :]

    row = lax.broadcasted_iota(jnp.int32, (Y, Z), 0)
    lane = lax.broadcasted_iota(jnp.int32, (Y, Z), 1)

    def near(plane, slot, s, xi):
        c = plane(xi)
        xm = plane(xi - 1) if xi > 0 else rx[slot, 0, s]
        xp = plane(xi + 1) if xi < X - 1 else rx[slot, 1, s]
        ym = jnp.where(row == 0, jnp.broadcast_to(ry[slot, 0, s, pl.ds(xi, 1), :], (Y, Z)), pltpu.roll(c, 1, 0))
        yp = jnp.where(row == Y - 1, jnp.broadcast_to(ry[slot, 1, s, pl.ds(xi, 1), :], (Y, Z)),
                       pltpu.roll(c, Y - 1, 0))
        zpair = jnp.where(
            row < Y // 2,
            jnp.broadcast_to(rz[slot, s, 1, pl.ds(xi, 1), :], (Y, Z)),
            jnp.broadcast_to(rz[slot, s, 0, pl.ds(xi, 1), :], (Y, Z)),
        ).T
        zm = jnp.where(lane == 0, zpair, pltpu.roll(c, 1, 1))
        zp = jnp.where(lane == Z - 1, zpair, pltpu.roll(c, Z - 1, 1))
        return c, (xm, xp, ym, yp, zm, zp)

    swap = pltpu.make_async_remote_copy(
        src_ref=st_ref, dst_ref=prev, send_sem=st_sem.at[0], recv_sem=st_sem.at[1],
        device_id=peers[4], device_id_type=MESH,
    )
    swap.start()

    for xi in range(X):
        put_faces(0, xi, kap_ref[xi])
    for c in copies(1, 0):
        c.start()
    for c in copies(1, 0):
        c.wait()
    for xi in range(X):
        kc, nb = near(lambda i: kap_ref[i], 1, 0, xi)
        for j in range(6):
            w_ref[j, xi] = (kc + nb[j]) * (0.5 * time_step)

    swap.wait()
    theta = ab_ref[2, 0]
    for s in range(S):
        for xi in range(X):
            if s == 0:
                scale = jnp.broadcast_to(rs_ref[pl.ds(xi, 1), :], (Z, Y)).T
                rhs = prev[xi].astype(jnp.float32) * scale
            else:
                rhs = cot_ref[xi]
            plane = rhs / theta
            dbuf[0, s, xi] = plane
            xo[s][xi] = jnp.zeros((Y, Z), jnp.float32)
            r_ref[s, xi] = rhs
            put_faces(s, xi, plane)
        for c in copies(0, s):
            c.start()

    def step(k, slot, final):
        nslot = 1 - slot
        a = ab_ref[0, k]
        b = ab_ref[1, k]
        for s in range(S):
            for c in copies(slot, s):
                c.wait()
            outgoing = copies(nslot, s)
            for xi in [0, X - 1] + list(range(1, X - 1)):
                if xi == 1:
                    for c in outgoing[:2]:
                        c.start()
                c, nb = near(lambda i: dbuf[slot, s, i], slot, s, xi)
                summed = w_ref[0, xi] * (c - nb[0])
                for j in range(1, 6):
                    summed = summed + w_ref[j, xi] * (c - nb[j])
                xn = xo[s][xi] + c
                xo[s][xi] = xn
                res = r_ref[s, xi] - (c + summed)
                r_ref[s, xi] = res
                if final:
                    put_faces(s, xi, xn)
                else:
                    nd = a * c + b * res
                    dbuf[nslot, s, xi] = nd
                    put_faces(s, xi, nd)
            for c in outgoing[2:]:
                c.start()

    def loop_step(k, carry):
        step(k, lax.rem(k, 2), False)
        return carry

    lax.fori_loop(0, CHEB - 1, loop_step, 0)
    step(CHEB - 1, (CHEB - 1) % 2, True)

    gslot = CHEB % 2
    for s in range(S):
        for c in copies(gslot, s):
            c.wait()
    for xi in range(X):
        c0, n0 = near(lambda i: xo[0][i], gslot, 0, xi)
        c1, n1 = near(lambda i: xo[1][i], gslot, 1, xi)
        summed = (c0 - n0[0]) * (c1 - n1[0])
        for j in range(1, 6):
            summed = summed + (c0 - n0[j]) * (c1 - n1[j])
        g_ref[xi] = (-0.5 * time_step) * summed


def body(conductivity, stored_state, row_scales, cotangent, upper_bound):
    X, Y, Z = conductivity.shape
    S = 2
    upper = upper_bound[0]
    theta = 0.5 * (upper + 1.0)
    delta = 0.5 * (upper - 1.0)
    sigma = theta / delta
    rho = 1.0 / sigma
    coefs = []
    for _ in range(CHEB):
        rho_next = 1.0 / (2.0 * sigma - rho)
        coefs.append((rho_next * rho, 2.0 * rho_next / delta))
        rho = rho_next
    ab = jnp.stack([
        jnp.stack([c[0] for c in coefs]),
        jnp.stack([c[1] for c in coefs]),
        jnp.broadcast_to(theta, (CHEB,)),
    ])

    ngx = lax.axis_size("gx")
    ngy = lax.axis_size("gy")
    f32 = jnp.float32
    vmem = pl.BlockSpec(memory_space=pltpu.VMEM)
    field = jax.ShapeDtypeStruct((X, Y, Z), f32)
    return pl.pallas_call(
        functools.partial(solve_kernel, ngx, ngy),
        out_shape=(field, field, field, jax.ShapeDtypeStruct((S, X, Y, Z), f32)),
        in_specs=[pl.BlockSpec(memory_space=pltpu.SMEM), vmem, vmem, vmem, vmem],
        out_specs=(vmem, vmem, vmem, vmem),
        scratch_shapes=[
            pltpu.VMEM((6, X, Y, Z), f32),
            pltpu.VMEM((X, Y, Z), stored_state.dtype),
            pltpu.VMEM((2, S, X, Y, Z), f32),
            pltpu.VMEM((2, S, Y, Z), f32),
            pltpu.VMEM((2, S, X, Z), f32),
            pltpu.VMEM((S, 2, X, Y), f32),
            pltpu.VMEM((2, 2, S, Y, Z), f32),
            pltpu.VMEM((2, 2, S, X, Z), f32),
            pltpu.VMEM((2, S, 2, X, Y), f32),
            pltpu.SemaphoreType.DMA((5, S, 2)),
            pltpu.SemaphoreType.DMA((5, S, 2)),
            pltpu.SemaphoreType.DMA((2,)),
        ],
        compiler_params=pltpu.CompilerParams(
            collective_id=0, has_side_effects=True, vmem_limit_bytes=60 * 1024 * 1024
        ),
    )(ab, conductivity, stored_state, row_scales, cotangent)


def solution(mesh):
    return jax.shard_map(
        body,
        mesh=mesh,
        in_specs=(
            P("gx", "gy", "pa"),
            P("gx", "gy", "pa"),
            P("gx", "gy"),
            P("gx", "gy", "pa"),
            P(),
        ),
        out_specs=(
            P("gx", "gy", "pa"),
            P("gx", "gy", "pa"),
            P("gx", "gy", "pa"),
            P(None, "gx", "gy", "pa"),
        ),
        check_vma=False,
    )
```

```python
import functools

import jax
import jax.numpy as jnp
from jax import lax
from jax.experimental import pallas as pl
from jax.experimental.pallas import tpu as pltpu
from jax.sharding import PartitionSpec as P

CHEB = 16

MESH = pl.DeviceIdType.MESH

time_step = 8.0


def solve_kernel(ngx, ngy, ab_ref, kap_ref, st_ref, rs_ref, cot_ref, g_ref, adj_ref, state_ref, r_ref,
                 w_ref, prev, dbuf, sx, sy, sz, rx, ry, rz, ax, ay, az, send_sem, recv_sem, st_sem):
    S = 2
    X, Y, Z = kap_ref.shape
    xo = (state_ref, adj_ref)
    gx = lax.axis_index("gx")
    gy = lax.axis_index("gy")
    pa = lax.axis_index("pa")
    gx_prev = lax.rem(gx + ngx - 1, ngx)
    gx_next = lax.rem(gx + 1, ngx)
    gy_prev = lax.rem(gy + ngy - 1, ngy)
    gy_next = lax.rem(gy + 1, ngy)
    partner = 1 - pa
    peers = ((gx_prev, gy, pa), (gx_next, gy, pa), (gx, gy_prev, pa), (gx, gy_next, pa), (gx, gy, partner))

    barrier = pltpu.get_barrier_semaphore()
    for dev in peers:
        pl.semaphore_signal(barrier, inc=1, device_id=dev, device_id_type=MESH)
    pl.semaphore_wait(barrier, len(peers))

    def copies(slot, s):
        plan = (
            (sx.at[0, s], rx.at[slot, 1, s], peers[0]),
            (sx.at[1, s], rx.at[slot, 0, s], peers[1]),
            (sy.at[0, s], ry.at[slot, 1, s], peers[2]),
            (sy.at[1, s], ry.at[slot, 0, s], peers[3]),
            (sz.at[s], rz.at[slot, s], peers[4]),
        )
        return [
            pltpu.make_async_remote_copy(
                src_ref=src, dst_ref=dst, send_sem=send_sem.at[i, s, slot], recv_sem=recv_sem.at[i, s, slot],
                device_id=dev, device_id_type=MESH,
            )
            for i, (src, dst, dev) in enumerate(plan)
        ]

    def put_faces(s, xi, plane):
        if xi == 0:
            sx[0, s] = plane
        if xi == X - 1:
            sx[1, s] = plane
        sy[0, s, pl.ds(xi, 1), :] = plane[0:1, :]
        sy[1, s, pl.ds(xi, 1), :] = plane[Y - 1:Y, :]
        t = plane.T
        sz[s, 0, pl.ds(xi, 1), :] = t[0:1, :]
        sz[s, 1, pl.ds(xi, 1), :] = t[Z - 1:Z, :]

    row = lax.broadcasted_iota(jnp.int32, (Y, Z), 0)
    lane = lax.broadcasted_iota(jnp.int32, (Y, Z), 1)

    def near(plane, hx, hy, hz, s, xi):
        c = plane(xi)
        xm = plane(xi - 1) if xi > 0 else hx[0, s]
        xp = plane(xi + 1) if xi < X - 1 else hx[1, s]
        ym = jnp.where(row == 0, jnp.broadcast_to(hy[0, s, pl.ds(xi, 1), :], (Y, Z)), pltpu.roll(c, 1, 0))
        yp = jnp.where(row == Y - 1, jnp.broadcast_to(hy[1, s, pl.ds(xi, 1), :], (Y, Z)),
                       pltpu.roll(c, Y - 1, 0))
        zpair = jnp.where(
            row < Y // 2,
            jnp.broadcast_to(hz[s, 1, pl.ds(xi, 1), :], (Y, Z)),
            jnp.broadcast_to(hz[s, 0, pl.ds(xi, 1), :], (Y, Z)),
        ).T
        zm = jnp.where(lane == 0, zpair, pltpu.roll(c, 1, 1))
        zp = jnp.where(lane == Z - 1, zpair, pltpu.roll(c, Z - 1, 1))
        return c, (xm, xp, ym, yp, zm, zp)

    swap = pltpu.make_async_remote_copy(
        src_ref=st_ref, dst_ref=prev, send_sem=st_sem.at[0], recv_sem=st_sem.at[1],
        device_id=peers[4], device_id_type=MESH,
    )
    swap.start()
    theta = ab_ref[2, 0]

    def start_solve(s):
        for xi in range(X):
            if s == 0:
                scale = jnp.broadcast_to(rs_ref[pl.ds(xi, 1), :], (Z, Y)).T
                rhs = prev[xi].astype(jnp.float32) * scale
            else:
                rhs = cot_ref[xi]
            plane = rhs / theta
            dbuf[0, s, xi] = plane
            xo[s][xi] = jnp.zeros((Y, Z), jnp.float32)
            r_ref[s, xi] = rhs
            put_faces(s, xi, plane)
        for c in copies(0, s):
            c.start()

    start_solve(1)

    for xi in range(X):
        put_faces(0, xi, kap_ref[xi])
    for c in copies(1, 0):
        c.start()
    for c in copies(1, 0):
        c.wait()
    for xi in range(X):
        kc, nb = near(lambda i: kap_ref[i], rx.at[1], ry.at[1], rz.at[1], 0, xi)
        for j in range(6):
            w_ref[j, xi] = (kc + nb[j]) * (0.5 * time_step)

    swap.wait()
    start_solve(0)
    for q in (ax, ay, az):
        q[...] = jnp.zeros(q.shape, jnp.float32)

    def step(k, slot, final):
        nslot = 1 - slot
        a = ab_ref[0, k]
        b = ab_ref[1, k]
        for s in (1, 0):
            for c in copies(slot, s):
                c.wait()
            ax[:, s] = ax[:, s] + rx[slot, :, s]
            ay[:, s] = ay[:, s] + ry[slot, :, s]
            az[s] = az[s] + rz[slot, s]
            outgoing = copies(nslot, s)
            for xi in [0, X - 1] + list(range(1, X - 1)):
                if xi == 1 and not final:
                    for c in outgoing[:2]:
                        c.start()
                c, nb = near(lambda i: dbuf[slot, s, i], rx.at[slot], ry.at[slot], rz.at[slot], s, xi)
                summed = w_ref[0, xi] * (c - nb[0])
                for j in range(1, 6):
                    summed = summed + w_ref[j, xi] * (c - nb[j])
                xo[s][xi] = xo[s][xi] + c
                res = r_ref[s, xi] - (c + summed)
                r_ref[s, xi] = res
                if not final:
                    nd = a * c + b * res
                    dbuf[nslot, s, xi] = nd
                    put_faces(s, xi, nd)
            if not final:
                for c in outgoing[2:]:
                    c.start()

    def loop_step(k, carry):
        step(k, lax.rem(k, 2), False)
        return carry

    lax.fori_loop(0, CHEB - 1, loop_step, 0)
    step(CHEB - 1, (CHEB - 1) % 2, True)

    for xi in range(X):
        c0, n0 = near(lambda i: xo[0][i], ax, ay, az, 0, xi)
        c1, n1 = near(lambda i: xo[1][i], ax, ay, az, 1, xi)
        summed = (c0 - n0[0]) * (c1 - n1[0])
        for j in range(1, 6):
            summed = summed + (c0 - n0[j]) * (c1 - n1[j])
        g_ref[xi] = (-0.5 * time_step) * summed


def body(conductivity, stored_state, row_scales, cotangent, upper_bound):
    X, Y, Z = conductivity.shape
    S = 2
    upper = upper_bound[0]
    theta = 0.5 * (upper + 1.0)
    delta = 0.5 * (upper - 1.0)
    sigma = theta / delta
    rho = 1.0 / sigma
    coefs = []
    for _ in range(CHEB):
        rho_next = 1.0 / (2.0 * sigma - rho)
        coefs.append((rho_next * rho, 2.0 * rho_next / delta))
        rho = rho_next
    ab = jnp.stack([
        jnp.stack([c[0] for c in coefs]),
        jnp.stack([c[1] for c in coefs]),
        jnp.broadcast_to(theta, (CHEB,)),
    ])

    ngx = lax.axis_size("gx")
    ngy = lax.axis_size("gy")
    f32 = jnp.float32
    vmem = pl.BlockSpec(memory_space=pltpu.VMEM)
    field = jax.ShapeDtypeStruct((X, Y, Z), f32)
    return pl.pallas_call(
        functools.partial(solve_kernel, ngx, ngy),
        out_shape=(field, field, field, jax.ShapeDtypeStruct((S, X, Y, Z), f32)),
        in_specs=[pl.BlockSpec(memory_space=pltpu.SMEM), vmem, vmem, vmem, vmem],
        out_specs=(vmem, vmem, vmem, vmem),
        scratch_shapes=[
            pltpu.VMEM((6, X, Y, Z), f32),
            pltpu.VMEM((X, Y, Z), stored_state.dtype),
            pltpu.VMEM((2, S, X, Y, Z), f32),
            pltpu.VMEM((2, S, Y, Z), f32),
            pltpu.VMEM((2, S, X, Z), f32),
            pltpu.VMEM((S, 2, X, Y), f32),
            pltpu.VMEM((2, 2, S, Y, Z), f32),
            pltpu.VMEM((2, 2, S, X, Z), f32),
            pltpu.VMEM((2, S, 2, X, Y), f32),
            pltpu.VMEM((2, S, Y, Z), f32),
            pltpu.VMEM((2, S, X, Z), f32),
            pltpu.VMEM((S, 2, X, Y), f32),
            pltpu.SemaphoreType.DMA((5, S, 2)),
            pltpu.SemaphoreType.DMA((5, S, 2)),
            pltpu.SemaphoreType.DMA((2,)),
        ],
        compiler_params=pltpu.CompilerParams(
            collective_id=0, has_side_effects=True, vmem_limit_bytes=60 * 1024 * 1024
        ),
    )(ab, conductivity, stored_state, row_scales, cotangent)


def solution(mesh):
    return jax.shard_map(
        body,
        mesh=mesh,
        in_specs=(
            P("gx", "gy", "pa"),
            P("gx", "gy", "pa"),
            P("gx", "gy"),
            P("gx", "gy", "pa"),
            P(),
        ),
        out_specs=(
            P("gx", "gy", "pa"),
            P("gx", "gy", "pa"),
            P("gx", "gy", "pa"),
            P(None, "gx", "gy", "pa"),
        ),
        check_vma=False,
    )
```

```python
import functools

import jax
import jax.numpy as jnp
from jax import lax
from jax.experimental import pallas as pl
from jax.experimental.pallas import tpu as pltpu
from jax.sharding import PartitionSpec as P

CHEB = 16

MESH = pl.DeviceIdType.MESH

time_step = 8.0


def solve_kernel(ngx, ngy, ab_ref, kap_ref, st_ref, rs_ref, cot_ref, g_ref, adj_ref, state_ref, r_ref,
                 w_ref, prev, dbuf, sx, sy, sz, rx, ry, rz, ax, ay, az, send_sem, recv_sem, st_sem):
    S = 2
    X, Y, Z = kap_ref.shape
    xo = (state_ref, adj_ref)
    gx = lax.axis_index("gx")
    gy = lax.axis_index("gy")
    pa = lax.axis_index("pa")
    gx_prev = lax.rem(gx + ngx - 1, ngx)
    gx_next = lax.rem(gx + 1, ngx)
    gy_prev = lax.rem(gy + ngy - 1, ngy)
    gy_next = lax.rem(gy + 1, ngy)
    partner = 1 - pa
    peers = ((gx_prev, gy, pa), (gx_next, gy, pa), (gx, gy_prev, pa), (gx, gy_next, pa), (gx, gy, partner))

    barrier = pltpu.get_barrier_semaphore()
    for dev in peers:
        pl.semaphore_signal(barrier, inc=1, device_id=dev, device_id_type=MESH)
    pl.semaphore_wait(barrier, len(peers))

    def copies(slot, s):
        plan = (
            (sx.at[0, s], rx.at[slot, 1, s], peers[0]),
            (sx.at[1, s], rx.at[slot, 0, s], peers[1]),
            (sy.at[0, s], ry.at[slot, 1, s], peers[2]),
            (sy.at[1, s], ry.at[slot, 0, s], peers[3]),
            (sz.at[s], rz.at[slot, s], peers[4]),
        )
        return [
            pltpu.make_async_remote_copy(
                src_ref=src, dst_ref=dst, send_sem=send_sem.at[i, s, slot], recv_sem=recv_sem.at[i, s, slot],
                device_id=dev, device_id_type=MESH,
            )
            for i, (src, dst, dev) in enumerate(plan)
        ]

    def put_faces(s, xi, plane):
        if xi == 0:
            sx[0, s] = plane
        if xi == X - 1:
            sx[1, s] = plane
        sy[0, s, pl.ds(xi, 1), :] = plane[0:1, :]
        sy[1, s, pl.ds(xi, 1), :] = plane[Y - 1:Y, :]
        t = plane.T
        sz[s, 0, pl.ds(xi, 1), :] = t[0:1, :]
        sz[s, 1, pl.ds(xi, 1), :] = t[Z - 1:Z, :]

    row = lax.broadcasted_iota(jnp.int32, (Y, Z), 0)
    lane = lax.broadcasted_iota(jnp.int32, (Y, Z), 1)

    def near(plane, hx, hy, hz, s, xi):
        c = plane(xi)
        xm = plane(xi - 1) if xi > 0 else hx[0, s]
        xp = plane(xi + 1) if xi < X - 1 else hx[1, s]
        ym = jnp.where(row == 0, jnp.broadcast_to(hy[0, s, pl.ds(xi, 1), :], (Y, Z)), pltpu.roll(c, 1, 0))
        yp = jnp.where(row == Y - 1, jnp.broadcast_to(hy[1, s, pl.ds(xi, 1), :], (Y, Z)),
                       pltpu.roll(c, Y - 1, 0))
        zpair = jnp.where(
            row < Y // 2,
            jnp.broadcast_to(hz[s, 1, pl.ds(xi, 1), :], (Y, Z)),
            jnp.broadcast_to(hz[s, 0, pl.ds(xi, 1), :], (Y, Z)),
        ).T
        zm = jnp.where(lane == 0, zpair, pltpu.roll(c, 1, 1))
        zp = jnp.where(lane == Z - 1, zpair, pltpu.roll(c, Z - 1, 1))
        return c, (xm, xp, ym, yp, zm, zp)

    swap = pltpu.make_async_remote_copy(
        src_ref=st_ref, dst_ref=prev, send_sem=st_sem.at[0], recv_sem=st_sem.at[1],
        device_id=peers[4], device_id_type=MESH,
    )
    swap.start()
    theta = ab_ref[2, 0]

    def start_solve(s):
        for xi in range(X):
            if s == 0:
                scale = jnp.broadcast_to(rs_ref[pl.ds(xi, 1), :], (Z, Y)).T
                rhs = prev[xi].astype(jnp.float32) * scale
            else:
                rhs = cot_ref[xi]
            plane = rhs / theta
            dbuf[0, s, xi] = plane
            xo[s][xi] = jnp.zeros((Y, Z), jnp.float32)
            r_ref[s, xi] = rhs
            put_faces(s, xi, plane)
        for c in copies(0, s):
            c.start()

    start_solve(1)

    for xi in range(X):
        put_faces(0, xi, kap_ref[xi])
    for c in copies(1, 0):
        c.start()
    for c in copies(1, 0):
        c.wait()
    for xi in range(X):
        kc, nb = near(lambda i: kap_ref[i], rx.at[1], ry.at[1], rz.at[1], 0, xi)
        for j in range(6):
            w_ref[j, xi] = (kc + nb[j]) * (0.5 * time_step)

    swap.wait()
    start_solve(0)
    for q in (ax, ay, az):
        q[...] = jnp.zeros(q.shape, jnp.float32)

    def step(k, slot, final):
        nslot = 1 - slot
        a = ab_ref[0, k]
        b = ab_ref[1, k]
        for s in (1, 0):
            incoming = copies(slot, s)
            for c in incoming[2:]:
                c.wait()
            ay[:, s] = ay[:, s] + ry[slot, :, s]
            az[s] = az[s] + rz[slot, s]
            for xi in list(range(1, X - 1)) + [0, X - 1]:
                if xi == 0:
                    for c in incoming[:2]:
                        c.wait()
                    ax[:, s] = ax[:, s] + rx[slot, :, s]
                c, nb = near(lambda i: dbuf[slot, s, i], rx.at[slot], ry.at[slot], rz.at[slot], s, xi)
                summed = w_ref[0, xi] * (c - nb[0])
                for j in range(1, 6):
                    summed = summed + w_ref[j, xi] * (c - nb[j])
                xo[s][xi] = xo[s][xi] + c
                res = r_ref[s, xi] - (c + summed)
                r_ref[s, xi] = res
                if not final:
                    nd = a * c + b * res
                    dbuf[nslot, s, xi] = nd
                    put_faces(s, xi, nd)
            if not final:
                for c in copies(nslot, s):
                    c.start()

    def loop_step(k, carry):
        step(k, lax.rem(k, 2), False)
        return carry

    lax.fori_loop(0, CHEB - 1, loop_step, 0)
    step(CHEB - 1, (CHEB - 1) % 2, True)

    for xi in range(X):
        c0, n0 = near(lambda i: xo[0][i], ax, ay, az, 0, xi)
        c1, n1 = near(lambda i: xo[1][i], ax, ay, az, 1, xi)
        summed = (c0 - n0[0]) * (c1 - n1[0])
        for j in range(1, 6):
            summed = summed + (c0 - n0[j]) * (c1 - n1[j])
        g_ref[xi] = (-0.5 * time_step) * summed


def body(conductivity, stored_state, row_scales, cotangent, upper_bound):
    X, Y, Z = conductivity.shape
    S = 2
    upper = upper_bound[0]
    theta = 0.5 * (upper + 1.0)
    delta = 0.5 * (upper - 1.0)
    sigma = theta / delta
    rho = 1.0 / sigma
    coefs = []
    for _ in range(CHEB):
        rho_next = 1.0 / (2.0 * sigma - rho)
        coefs.append((rho_next * rho, 2.0 * rho_next / delta))
        rho = rho_next
    ab = jnp.stack([
        jnp.stack([c[0] for c in coefs]),
        jnp.stack([c[1] for c in coefs]),
        jnp.broadcast_to(theta, (CHEB,)),
    ])

    ngx = lax.axis_size("gx")
    ngy = lax.axis_size("gy")
    f32 = jnp.float32
    vmem = pl.BlockSpec(memory_space=pltpu.VMEM)
    field = jax.ShapeDtypeStruct((X, Y, Z), f32)
    return pl.pallas_call(
        functools.partial(solve_kernel, ngx, ngy),
        out_shape=(field, field, field, jax.ShapeDtypeStruct((S, X, Y, Z), f32)),
        in_specs=[pl.BlockSpec(memory_space=pltpu.SMEM), vmem, vmem, vmem, vmem],
        out_specs=(vmem, vmem, vmem, vmem),
        scratch_shapes=[
            pltpu.VMEM((6, X, Y, Z), f32),
            pltpu.VMEM((X, Y, Z), stored_state.dtype),
            pltpu.VMEM((2, S, X, Y, Z), f32),
            pltpu.VMEM((2, S, Y, Z), f32),
            pltpu.VMEM((2, S, X, Z), f32),
            pltpu.VMEM((S, 2, X, Y), f32),
            pltpu.VMEM((2, 2, S, Y, Z), f32),
            pltpu.VMEM((2, 2, S, X, Z), f32),
            pltpu.VMEM((2, S, 2, X, Y), f32),
            pltpu.VMEM((2, S, Y, Z), f32),
            pltpu.VMEM((2, S, X, Z), f32),
            pltpu.VMEM((S, 2, X, Y), f32),
            pltpu.SemaphoreType.DMA((5, S, 2)),
            pltpu.SemaphoreType.DMA((5, S, 2)),
            pltpu.SemaphoreType.DMA((2,)),
        ],
        compiler_params=pltpu.CompilerParams(
            collective_id=0, has_side_effects=True, vmem_limit_bytes=60 * 1024 * 1024
        ),
    )(ab, conductivity, stored_state, row_scales, cotangent)


def solution(mesh):
    return jax.shard_map(
        body,
        mesh=mesh,
        in_specs=(
            P("gx", "gy", "pa"),
            P("gx", "gy", "pa"),
            P("gx", "gy"),
            P("gx", "gy", "pa"),
            P(),
        ),
        out_specs=(
            P("gx", "gy", "pa"),
            P("gx", "gy", "pa"),
            P("gx", "gy", "pa"),
            P(None, "gx", "gy", "pa"),
        ),
        check_vma=False,
    )
```

```python
import functools

import jax
import jax.numpy as jnp
from jax import lax
from jax.experimental import pallas as pl
from jax.experimental.pallas import tpu as pltpu
from jax.sharding import PartitionSpec as P

CHEB = 16

MESH = pl.DeviceIdType.MESH

time_step = 8.0


def solve_kernel(ngx, ngy, ab_ref, kap_ref, st_ref, rs_ref, cot_ref, g_ref, adj_ref, state_ref, r_ref,
                 w_ref, prev, dbuf, sx, sy, sz, rx, ry, rz, ax, ay, az, send_sem, recv_sem, st_sem):
    S = 2
    X, Y, Z = kap_ref.shape
    xo = (state_ref, adj_ref)
    gx = lax.axis_index("gx")
    gy = lax.axis_index("gy")
    pa = lax.axis_index("pa")
    gx_prev = lax.rem(gx + ngx - 1, ngx)
    gx_next = lax.rem(gx + 1, ngx)
    gy_prev = lax.rem(gy + ngy - 1, ngy)
    gy_next = lax.rem(gy + 1, ngy)
    partner = 1 - pa
    peers = ((gx_prev, gy, pa), (gx_next, gy, pa), (gx, gy_prev, pa), (gx, gy_next, pa), (gx, gy, partner))

    barrier = pltpu.get_barrier_semaphore()
    for dev in peers:
        pl.semaphore_signal(barrier, inc=1, device_id=dev, device_id_type=MESH)
    pl.semaphore_wait(barrier, len(peers))

    def copies(slot, s):
        plan = (
            (sx.at[0, s], rx.at[slot, 1, s], peers[0]),
            (sx.at[1, s], rx.at[slot, 0, s], peers[1]),
            (sy.at[0, s], ry.at[slot, 1, s], peers[2]),
            (sy.at[1, s], ry.at[slot, 0, s], peers[3]),
            (sz.at[s], rz.at[slot, s], peers[4]),
        )
        return [
            pltpu.make_async_remote_copy(
                src_ref=src, dst_ref=dst, send_sem=send_sem.at[i, s, slot], recv_sem=recv_sem.at[i, s, slot],
                device_id=dev, device_id_type=MESH,
            )
            for i, (src, dst, dev) in enumerate(plan)
        ]

    def put_faces(s, xi, plane):
        if xi == 0:
            sx[0, s] = plane
        if xi == X - 1:
            sx[1, s] = plane
        sy[0, s, pl.ds(xi, 1), :] = plane[0:1, :]
        sy[1, s, pl.ds(xi, 1), :] = plane[Y - 1:Y, :]
        t = plane.T
        sz[s, 0, pl.ds(xi, 1), :] = t[0:1, :]
        sz[s, 1, pl.ds(xi, 1), :] = t[Z - 1:Z, :]

    row = lax.broadcasted_iota(jnp.int32, (Y, Z), 0)
    lane = lax.broadcasted_iota(jnp.int32, (Y, Z), 1)
    CH = 32
    crow = lax.broadcasted_iota(jnp.int32, (CH, Z), 0)
    clane = lax.broadcasted_iota(jnp.int32, (CH, Z), 1)

    def near(plane, hx, hy, hz, s, xi):
        c = plane(xi)
        xm = plane(xi - 1) if xi > 0 else hx[0, s]
        xp = plane(xi + 1) if xi < X - 1 else hx[1, s]
        ym = jnp.where(row == 0, jnp.broadcast_to(hy[0, s, pl.ds(xi, 1), :], (Y, Z)), pltpu.roll(c, 1, 0))
        yp = jnp.where(row == Y - 1, jnp.broadcast_to(hy[1, s, pl.ds(xi, 1), :], (Y, Z)),
                       pltpu.roll(c, Y - 1, 0))
        zpair = jnp.where(
            row < Y // 2,
            jnp.broadcast_to(hz[s, 1, pl.ds(xi, 1), :], (Y, Z)),
            jnp.broadcast_to(hz[s, 0, pl.ds(xi, 1), :], (Y, Z)),
        ).T
        zm = jnp.where(lane == 0, zpair, pltpu.roll(c, 1, 1))
        zp = jnp.where(lane == Z - 1, zpair, pltpu.roll(c, Z - 1, 1))
        return c, (xm, xp, ym, yp, zm, zp)

    swap = pltpu.make_async_remote_copy(
        src_ref=st_ref, dst_ref=prev, send_sem=st_sem.at[0], recv_sem=st_sem.at[1],
        device_id=peers[4], device_id_type=MESH,
    )
    swap.start()
    theta = ab_ref[2, 0]

    def start_solve(s):
        for xi in range(X):
            if s == 0:
                scale = jnp.broadcast_to(rs_ref[pl.ds(xi, 1), :], (Z, Y)).T
                rhs = prev[xi].astype(jnp.float32) * scale
            else:
                rhs = cot_ref[xi]
            plane = rhs / theta
            dbuf[0, s, xi] = plane
            xo[s][xi] = jnp.zeros((Y, Z), jnp.float32)
            r_ref[s, xi] = rhs
            put_faces(s, xi, plane)
        for c in copies(0, s):
            c.start()

    start_solve(1)

    for xi in range(X):
        put_faces(0, xi, kap_ref[xi])
    for c in copies(1, 0):
        c.start()
    for c in copies(1, 0):
        c.wait()
    for xi in range(X):
        kc, nb = near(lambda i: kap_ref[i], rx.at[1], ry.at[1], rz.at[1], 0, xi)
        for j in range(6):
            w_ref[j, xi] = (kc + nb[j]) * (0.5 * time_step)

    swap.wait()
    start_solve(0)
    for q in (ax, ay, az):
        q[...] = jnp.zeros(q.shape, jnp.float32)

    def step(k, slot, final):
        nslot = 1 - slot
        a = ab_ref[0, k]
        b = ab_ref[1, k]
        for s in (1, 0):
            incoming = copies(slot, s)
            for c in incoming[2:]:
                c.wait()
            ay[:, s] = ay[:, s] + ry[slot, :, s]
            az[s] = az[s] + rz[slot, s]
            for xi in list(range(1, X - 1)) + [0, X - 1]:
                if xi == 0:
                    for c in incoming[:2]:
                        c.wait()
                    ax[:, s] = ax[:, s] + rx[slot, :, s]
                zpair = jnp.where(
                    row < Y // 2,
                    jnp.broadcast_to(rz[slot, s, 1, pl.ds(xi, 1), :], (Y, Z)),
                    jnp.broadcast_to(rz[slot, s, 0, pl.ds(xi, 1), :], (Y, Z)),
                ).T
                for q in range(Y // CH):
                    rows = pl.ds(q * CH, CH)
                    c = dbuf[slot, s, xi, rows, :]
                    xm = dbuf[slot, s, xi - 1, rows, :] if xi > 0 else rx[slot, 0, s, rows, :]
                    xp = dbuf[slot, s, xi + 1, rows, :] if xi < X - 1 else rx[slot, 1, s, rows, :]
                    above = ry[slot, 0, s, pl.ds(xi, 1), :] if q == 0 else dbuf[slot, s, xi, pl.ds(q * CH - 1, 1), :]
                    below = (ry[slot, 1, s, pl.ds(xi, 1), :] if q == Y // CH - 1
                             else dbuf[slot, s, xi, pl.ds(q * CH + CH, 1), :])
                    ym = jnp.where(crow == 0, jnp.broadcast_to(above, (CH, Z)), pltpu.roll(c, 1, 0))
                    yp = jnp.where(crow == CH - 1, jnp.broadcast_to(below, (CH, Z)), pltpu.roll(c, CH - 1, 0))
                    zq = zpair[q * CH:(q + 1) * CH]
                    zm = jnp.where(clane == 0, zq, pltpu.roll(c, 1, 1))
                    zp = jnp.where(clane == Z - 1, zq, pltpu.roll(c, Z - 1, 1))
                    nb = (xm, xp, ym, yp, zm, zp)
                    summed = w_ref[0, xi, rows, :] * (c - nb[0])
                    for j in range(1, 6):
                        summed = summed + w_ref[j, xi, rows, :] * (c - nb[j])
                    xo[s][xi, rows, :] = xo[s][xi, rows, :] + c
                    res = r_ref[s, xi, rows, :] - (c + summed)
                    r_ref[s, xi, rows, :] = res
                    if not final:
                        dbuf[nslot, s, xi, rows, :] = a * c + b * res
                if not final:
                    put_faces(s, xi, dbuf[nslot, s, xi])
            if not final:
                for c in copies(nslot, s):
                    c.start()

    def loop_step(k, carry):
        step(k, lax.rem(k, 2), False)
        return carry

    lax.fori_loop(0, CHEB - 1, loop_step, 0)
    step(CHEB - 1, (CHEB - 1) % 2, True)

    for xi in range(X):
        c0, n0 = near(lambda i: xo[0][i], ax, ay, az, 0, xi)
        c1, n1 = near(lambda i: xo[1][i], ax, ay, az, 1, xi)
        summed = (c0 - n0[0]) * (c1 - n1[0])
        for j in range(1, 6):
            summed = summed + (c0 - n0[j]) * (c1 - n1[j])
        g_ref[xi] = (-0.5 * time_step) * summed


def body(conductivity, stored_state, row_scales, cotangent, upper_bound):
    X, Y, Z = conductivity.shape
    S = 2
    upper = upper_bound[0]
    theta = 0.5 * (upper + 1.0)
    delta = 0.5 * (upper - 1.0)
    sigma = theta / delta
    rho = 1.0 / sigma
    coefs = []
    for _ in range(CHEB):
        rho_next = 1.0 / (2.0 * sigma - rho)
        coefs.append((rho_next * rho, 2.0 * rho_next / delta))
        rho = rho_next
    ab = jnp.stack([
        jnp.stack([c[0] for c in coefs]),
        jnp.stack([c[1] for c in coefs]),
        jnp.broadcast_to(theta, (CHEB,)),
    ])

    ngx = lax.axis_size("gx")
    ngy = lax.axis_size("gy")
    f32 = jnp.float32
    vmem = pl.BlockSpec(memory_space=pltpu.VMEM)
    field = jax.ShapeDtypeStruct((X, Y, Z), f32)
    return pl.pallas_call(
        functools.partial(solve_kernel, ngx, ngy),
        out_shape=(field, field, field, jax.ShapeDtypeStruct((S, X, Y, Z), f32)),
        in_specs=[pl.BlockSpec(memory_space=pltpu.SMEM), vmem, vmem, vmem, vmem],
        out_specs=(vmem, vmem, vmem, vmem),
        scratch_shapes=[
            pltpu.VMEM((6, X, Y, Z), f32),
            pltpu.VMEM((X, Y, Z), stored_state.dtype),
            pltpu.VMEM((2, S, X, Y, Z), f32),
            pltpu.VMEM((2, S, Y, Z), f32),
            pltpu.VMEM((2, S, X, Z), f32),
            pltpu.VMEM((S, 2, X, Y), f32),
            pltpu.VMEM((2, 2, S, Y, Z), f32),
            pltpu.VMEM((2, 2, S, X, Z), f32),
            pltpu.VMEM((2, S, 2, X, Y), f32),
            pltpu.VMEM((2, S, Y, Z), f32),
            pltpu.VMEM((2, S, X, Z), f32),
            pltpu.VMEM((S, 2, X, Y), f32),
            pltpu.SemaphoreType.DMA((5, S, 2)),
            pltpu.SemaphoreType.DMA((5, S, 2)),
            pltpu.SemaphoreType.DMA((2,)),
        ],
        compiler_params=pltpu.CompilerParams(
            collective_id=0, has_side_effects=True, vmem_limit_bytes=60 * 1024 * 1024
        ),
    )(ab, conductivity, stored_state, row_scales, cotangent)


def solution(mesh):
    return jax.shard_map(
        body,
        mesh=mesh,
        in_specs=(
            P("gx", "gy", "pa"),
            P("gx", "gy", "pa"),
            P("gx", "gy"),
            P("gx", "gy", "pa"),
            P(),
        ),
        out_specs=(
            P("gx", "gy", "pa"),
            P("gx", "gy", "pa"),
            P("gx", "gy", "pa"),
            P(None, "gx", "gy", "pa"),
        ),
        check_vma=False,
    )
```

```python
import functools

import jax
import jax.numpy as jnp
from jax import lax
from jax.experimental import pallas as pl
from jax.experimental.pallas import tpu as pltpu
from jax.sharding import PartitionSpec as P

CHEB = 16

MESH = pl.DeviceIdType.MESH

time_step = 8.0


def solve_kernel(ngx, ngy, ab_ref, kap_ref, st_ref, rs_ref, cot_ref, g_ref, adj_ref, state_ref, r_ref,
                 w_ref, prev, dbuf, sx, sy, sz, rx, ry, rz, ax, ay, az, send_sem, recv_sem, st_sem):
    S = 2
    X, Y, Z = kap_ref.shape
    xo = (state_ref, adj_ref)
    gx = lax.axis_index("gx")
    gy = lax.axis_index("gy")
    pa = lax.axis_index("pa")
    gx_prev = lax.rem(gx + ngx - 1, ngx)
    gx_next = lax.rem(gx + 1, ngx)
    gy_prev = lax.rem(gy + ngy - 1, ngy)
    gy_next = lax.rem(gy + 1, ngy)
    partner = 1 - pa
    peers = ((gx_prev, gy, pa), (gx_next, gy, pa), (gx, gy_prev, pa), (gx, gy_next, pa), (gx, gy, partner))

    barrier = pltpu.get_barrier_semaphore()
    for dev in peers:
        pl.semaphore_signal(barrier, inc=1, device_id=dev, device_id_type=MESH)
    pl.semaphore_wait(barrier, len(peers))

    def copies(slot, s):
        plan = (
            (sx.at[0, s], rx.at[slot, 1, s], peers[0]),
            (sx.at[1, s], rx.at[slot, 0, s], peers[1]),
            (sy.at[0, s], ry.at[slot, 1, s], peers[2]),
            (sy.at[1, s], ry.at[slot, 0, s], peers[3]),
            (sz.at[s], rz.at[slot, s], peers[4]),
        )
        return [
            pltpu.make_async_remote_copy(
                src_ref=src, dst_ref=dst, send_sem=send_sem.at[i, s, slot], recv_sem=recv_sem.at[i, s, slot],
                device_id=dev, device_id_type=MESH,
            )
            for i, (src, dst, dev) in enumerate(plan)
        ]

    def put_faces(s, xi, plane):
        if xi == 0:
            sx[0, s] = plane
        if xi == X - 1:
            sx[1, s] = plane
        sy[0, s, pl.ds(xi, 1), :] = plane[0:1, :]
        sy[1, s, pl.ds(xi, 1), :] = plane[Y - 1:Y, :]
        t = plane.T
        sz[s, 0, pl.ds(xi, 1), :] = t[0:1, :]
        sz[s, 1, pl.ds(xi, 1), :] = t[Z - 1:Z, :]

    row = lax.broadcasted_iota(jnp.int32, (Y, Z), 0)
    lane = lax.broadcasted_iota(jnp.int32, (Y, Z), 1)
    CH = 32
    crow = lax.broadcasted_iota(jnp.int32, (CH, Z), 0)
    clane = lax.broadcasted_iota(jnp.int32, (CH, Z), 1)

    def near(plane, hx, hy, hz, s, xi):
        c = plane(xi)
        xm = plane(xi - 1) if xi > 0 else hx[0, s]
        xp = plane(xi + 1) if xi < X - 1 else hx[1, s]
        ym = jnp.where(row == 0, jnp.broadcast_to(hy[0, s, pl.ds(xi, 1), :], (Y, Z)), pltpu.roll(c, 1, 0))
        yp = jnp.where(row == Y - 1, jnp.broadcast_to(hy[1, s, pl.ds(xi, 1), :], (Y, Z)),
                       pltpu.roll(c, Y - 1, 0))
        zpair = jnp.where(
            row < Y // 2,
            jnp.broadcast_to(hz[s, 1, pl.ds(xi, 1), :], (Y, Z)),
            jnp.broadcast_to(hz[s, 0, pl.ds(xi, 1), :], (Y, Z)),
        ).T
        zm = jnp.where(lane == 0, zpair, pltpu.roll(c, 1, 1))
        zp = jnp.where(lane == Z - 1, zpair, pltpu.roll(c, Z - 1, 1))
        return c, (xm, xp, ym, yp, zm, zp)

    swap = pltpu.make_async_remote_copy(
        src_ref=st_ref, dst_ref=prev, send_sem=st_sem.at[0], recv_sem=st_sem.at[1],
        device_id=peers[4], device_id_type=MESH,
    )
    swap.start()
    theta = ab_ref[2, 0]

    def start_solve(s):
        for xi in range(X):
            if s == 0:
                scale = jnp.broadcast_to(rs_ref[pl.ds(xi, 1), :], (Z, Y)).T
                rhs = prev[xi].astype(jnp.float32) * scale
            else:
                rhs = cot_ref[xi]
            plane = rhs / theta
            dbuf[0, s, xi] = plane
            xo[s][xi] = jnp.zeros((Y, Z), jnp.float32)
            r_ref[s, xi] = rhs
            put_faces(s, xi, plane)
        for c in copies(0, s):
            c.start()

    start_solve(1)

    for xi in range(X):
        put_faces(0, xi, kap_ref[xi])
    for c in copies(1, 0):
        c.start()
    for c in copies(1, 0):
        c.wait()
    for xi in range(X):
        kc, nb = near(lambda i: kap_ref[i], rx.at[1], ry.at[1], rz.at[1], 0, xi)
        for j in range(6):
            w_ref[j, xi] = (kc + nb[j]) * (0.5 * time_step)

    swap.wait()
    start_solve(0)
    for q in (ax, ay, az):
        q[...] = jnp.zeros(q.shape, jnp.float32)

    def step(k, slot, final):
        nslot = 1 - slot
        a = ab_ref[0, k]
        b = ab_ref[1, k]
        for s in (1, 0):
            incoming = copies(slot, s)
            for c in incoming[2:]:
                c.wait()
            ay[:, s] = ay[:, s] + ry[slot, :, s]
            az[s] = az[s] + rz[slot, s]
            for xi in list(range(1, X - 1)) + [0, X - 1]:
                if xi == 0:
                    for c in incoming[:2]:
                        c.wait()
                    ax[:, s] = ax[:, s] + rx[slot, :, s]
                zpair = jnp.where(
                    row < Y // 2,
                    jnp.broadcast_to(rz[slot, s, 1, pl.ds(xi, 1), :], (Y, Z)),
                    jnp.broadcast_to(rz[slot, s, 0, pl.ds(xi, 1), :], (Y, Z)),
                ).T
                for q in range(Y // CH):
                    rows = pl.ds(q * CH, CH)
                    c = dbuf[slot, s, xi, rows, :]
                    xm = dbuf[slot, s, xi - 1, rows, :] if xi > 0 else rx[slot, 0, s, rows, :]
                    xp = dbuf[slot, s, xi + 1, rows, :] if xi < X - 1 else rx[slot, 1, s, rows, :]
                    above = ry[slot, 0, s, pl.ds(xi, 1), :] if q == 0 else dbuf[slot, s, xi, pl.ds(q * CH - 1, 1), :]
                    below = (ry[slot, 1, s, pl.ds(xi, 1), :] if q == Y // CH - 1
                             else dbuf[slot, s, xi, pl.ds(q * CH + CH, 1), :])
                    ym = jnp.where(crow == 0, jnp.broadcast_to(above, (CH, Z)), pltpu.roll(c, 1, 0))
                    yp = jnp.where(crow == CH - 1, jnp.broadcast_to(below, (CH, Z)), pltpu.roll(c, CH - 1, 0))
                    zq = zpair[q * CH:(q + 1) * CH]
                    zm = jnp.where(clane == 0, zq, pltpu.roll(c, 1, 1))
                    zp = jnp.where(clane == Z - 1, zq, pltpu.roll(c, Z - 1, 1))
                    nb = (xm, xp, ym, yp, zm, zp)
                    summed = w_ref[0, xi, rows, :] * (c - nb[0])
                    for j in range(1, 6):
                        summed = summed + w_ref[j, xi, rows, :] * (c - nb[j])
                    xo[s][xi, rows, :] = xo[s][xi, rows, :] + c
                    res = r_ref[s, xi, rows, :] - (c + summed)
                    r_ref[s, xi, rows, :] = res
                    if not final:
                        dbuf[nslot, s, xi, rows, :] = a * c + b * res
                if not final:
                    put_faces(s, xi, dbuf[nslot, s, xi])
            if not final:
                outgoing = copies(nslot, s)
                for i in (4, 2, 3, 0, 1):
                    outgoing[i].start()

    def loop_step(k, carry):
        step(k, lax.rem(k, 2), False)
        return carry

    lax.fori_loop(0, CHEB - 1, loop_step, 0)
    step(CHEB - 1, (CHEB - 1) % 2, True)

    for xi in range(X):
        c0, n0 = near(lambda i: xo[0][i], ax, ay, az, 0, xi)
        c1, n1 = near(lambda i: xo[1][i], ax, ay, az, 1, xi)
        summed = (c0 - n0[0]) * (c1 - n1[0])
        for j in range(1, 6):
            summed = summed + (c0 - n0[j]) * (c1 - n1[j])
        g_ref[xi] = (-0.5 * time_step) * summed


def body(conductivity, stored_state, row_scales, cotangent, upper_bound):
    X, Y, Z = conductivity.shape
    S = 2
    upper = upper_bound[0]
    theta = 0.5 * (upper + 1.0)
    delta = 0.5 * (upper - 1.0)
    sigma = theta / delta
    rho = 1.0 / sigma
    coefs = []
    for _ in range(CHEB):
        rho_next = 1.0 / (2.0 * sigma - rho)
        coefs.append((rho_next * rho, 2.0 * rho_next / delta))
        rho = rho_next
    ab = jnp.stack([
        jnp.stack([c[0] for c in coefs]),
        jnp.stack([c[1] for c in coefs]),
        jnp.broadcast_to(theta, (CHEB,)),
    ])

    ngx = lax.axis_size("gx")
    ngy = lax.axis_size("gy")
    f32 = jnp.float32
    vmem = pl.BlockSpec(memory_space=pltpu.VMEM)
    field = jax.ShapeDtypeStruct((X, Y, Z), f32)
    return pl.pallas_call(
        functools.partial(solve_kernel, ngx, ngy),
        out_shape=(field, field, field, jax.ShapeDtypeStruct((S, X, Y, Z), f32)),
        in_specs=[pl.BlockSpec(memory_space=pltpu.SMEM), vmem, vmem, vmem, vmem],
        out_specs=(vmem, vmem, vmem, vmem),
        scratch_shapes=[
            pltpu.VMEM((6, X, Y, Z), f32),
            pltpu.VMEM((X, Y, Z), stored_state.dtype),
            pltpu.VMEM((2, S, X, Y, Z), f32),
            pltpu.VMEM((2, S, Y, Z), f32),
            pltpu.VMEM((2, S, X, Z), f32),
            pltpu.VMEM((S, 2, X, Y), f32),
            pltpu.VMEM((2, 2, S, Y, Z), f32),
            pltpu.VMEM((2, 2, S, X, Z), f32),
            pltpu.VMEM((2, S, 2, X, Y), f32),
            pltpu.VMEM((2, S, Y, Z), f32),
            pltpu.VMEM((2, S, X, Z), f32),
            pltpu.VMEM((S, 2, X, Y), f32),
            pltpu.SemaphoreType.DMA((5, S, 2)),
            pltpu.SemaphoreType.DMA((5, S, 2)),
            pltpu.SemaphoreType.DMA((2,)),
        ],
        compiler_params=pltpu.CompilerParams(
            collective_id=0, has_side_effects=True, vmem_limit_bytes=60 * 1024 * 1024
        ),
    )(ab, conductivity, stored_state, row_scales, cotangent)


def solution(mesh):
    return jax.shard_map(
        body,
        mesh=mesh,
        in_specs=(
            P("gx", "gy", "pa"),
            P("gx", "gy", "pa"),
            P("gx", "gy"),
            P("gx", "gy", "pa"),
            P(),
        ),
        out_specs=(
            P("gx", "gy", "pa"),
            P("gx", "gy", "pa"),
            P("gx", "gy", "pa"),
            P(None, "gx", "gy", "pa"),
        ),
        check_vma=False,
    )
```

```python
import functools

import jax
import jax.numpy as jnp
from jax import lax
from jax.experimental import pallas as pl
from jax.experimental.pallas import tpu as pltpu
from jax.sharding import PartitionSpec as P

CHEB = 16

MESH = pl.DeviceIdType.MESH

time_step = 8.0


def solve_kernel(ngx, ngy, ab_ref, kap_ref, st_ref, rs_ref, cot_ref, g_ref, adj_ref, state_ref, r_ref,
                 w_ref, prev, dbuf, sx, sy, sz, rx, ry, rz, ax, ay, az, syi, szi, ryi, rzi, ayi, azi,
                 send_sem, recv_sem, st_sem):
    S = 2
    X, Y, Z = kap_ref.shape
    xo = (state_ref, adj_ref)
    gx = lax.axis_index("gx")
    gy = lax.axis_index("gy")
    pa = lax.axis_index("pa")
    gx_prev = lax.rem(gx + ngx - 1, ngx)
    gx_next = lax.rem(gx + 1, ngx)
    gy_prev = lax.rem(gy + ngy - 1, ngy)
    gy_next = lax.rem(gy + 1, ngy)
    partner = 1 - pa
    peers = ((gx_prev, gy, pa), (gx_next, gy, pa), (gx, gy_prev, pa), (gx, gy_next, pa), (gx, gy, partner))

    barrier = pltpu.get_barrier_semaphore()
    for dev in peers:
        pl.semaphore_signal(barrier, inc=1, device_id=dev, device_id_type=MESH)
    pl.semaphore_wait(barrier, len(peers))

    def copies(slot, s):
        plan = (
            (sx.at[0, s], rx.at[slot, 1, s], peers[0]),
            (sx.at[1, s], rx.at[slot, 0, s], peers[1]),
            (sy.at[0, s], ry.at[slot, 1, s], peers[2]),
            (sy.at[1, s], ry.at[slot, 0, s], peers[3]),
            (sz.at[s], rz.at[slot, s], peers[4]),
            (syi.at[0, s], ryi.at[slot, 1, s], peers[2]),
            (syi.at[1, s], ryi.at[slot, 0, s], peers[3]),
            (szi.at[s], rzi.at[slot, s], peers[4]),
        )
        return [
            pltpu.make_async_remote_copy(
                src_ref=src, dst_ref=dst, send_sem=send_sem.at[i, s, slot], recv_sem=recv_sem.at[i, s, slot],
                device_id=dev, device_id_type=MESH,
            )
            for i, (src, dst, dev) in enumerate(plan)
        ]

    def put_faces(s, xi, plane):
        if xi == 0:
            sx[0, s] = plane
        if xi == X - 1:
            sx[1, s] = plane
        fy, fz = (sy, sz) if xi in (0, X - 1) else (syi, szi)
        fy[0, s, pl.ds(xi, 1), :] = plane[0:1, :]
        fy[1, s, pl.ds(xi, 1), :] = plane[Y - 1:Y, :]
        t = plane.T
        fz[s, 0, pl.ds(xi, 1), :] = t[0:1, :]
        fz[s, 1, pl.ds(xi, 1), :] = t[Z - 1:Z, :]

    row = lax.broadcasted_iota(jnp.int32, (Y, Z), 0)
    lane = lax.broadcasted_iota(jnp.int32, (Y, Z), 1)

    def near(plane, hx, hy, hz, s, xi):
        c = plane(xi)
        xm = plane(xi - 1) if xi > 0 else hx[0, s]
        xp = plane(xi + 1) if xi < X - 1 else hx[1, s]
        ym = jnp.where(row == 0, jnp.broadcast_to(hy[0, s, pl.ds(xi, 1), :], (Y, Z)), pltpu.roll(c, 1, 0))
        yp = jnp.where(row == Y - 1, jnp.broadcast_to(hy[1, s, pl.ds(xi, 1), :], (Y, Z)),
                       pltpu.roll(c, Y - 1, 0))
        zpair = jnp.where(
            row < Y // 2,
            jnp.broadcast_to(hz[s, 1, pl.ds(xi, 1), :], (Y, Z)),
            jnp.broadcast_to(hz[s, 0, pl.ds(xi, 1), :], (Y, Z)),
        ).T
        zm = jnp.where(lane == 0, zpair, pltpu.roll(c, 1, 1))
        zp = jnp.where(lane == Z - 1, zpair, pltpu.roll(c, Z - 1, 1))
        return c, (xm, xp, ym, yp, zm, zp)

    swap = pltpu.make_async_remote_copy(
        src_ref=st_ref, dst_ref=prev, send_sem=st_sem.at[0], recv_sem=st_sem.at[1],
        device_id=peers[4], device_id_type=MESH,
    )
    swap.start()
    theta = ab_ref[2, 0]
    for q in (sy, sz, syi, szi):
        q[...] = jnp.zeros(q.shape, jnp.float32)

    def start_solve(s):
        for xi in range(X):
            if s == 0:
                scale = jnp.broadcast_to(rs_ref[pl.ds(xi, 1), :], (Z, Y)).T
                rhs = prev[xi].astype(jnp.float32) * scale
            else:
                rhs = cot_ref[xi]
            plane = rhs / theta
            dbuf[0, s, xi] = plane
            xo[s][xi] = jnp.zeros((Y, Z), jnp.float32)
            r_ref[s, xi] = rhs
            put_faces(s, xi, plane)
        for c in copies(0, s):
            c.start()

    start_solve(1)

    for xi in range(X):
        put_faces(0, xi, kap_ref[xi])
    for c in copies(1, 0):
        c.start()
    for c in copies(1, 0):
        c.wait()
    for xi in range(X):
        hy, hz = (ry, rz) if xi in (0, X - 1) else (ryi, rzi)
        kc, nb = near(lambda i: kap_ref[i], rx.at[1], hy.at[1], hz.at[1], 0, xi)
        for j in range(6):
            w_ref[j, xi] = (kc + nb[j]) * (0.5 * time_step)

    swap.wait()
    start_solve(0)
    for q in (ax, ay, az, ayi, azi):
        q[...] = jnp.zeros(q.shape, jnp.float32)

    def step(k, slot, final):
        nslot = 1 - slot
        a = ab_ref[0, k]
        b = ab_ref[1, k]
        for s in (1, 0):
            incoming = copies(slot, s)
            outgoing = copies(nslot, s)
            for c in incoming[5:]:
                c.wait()
            ayi[:, s] = ayi[:, s] + ryi[slot, :, s]
            azi[s] = azi[s] + rzi[slot, s]
            for xi in list(range(1, X - 1)) + [0, X - 1]:
                if xi == 0:
                    if not final:
                        for c in outgoing[5:]:
                            c.start()
                    for c in incoming[:5]:
                        c.wait()
                    ax[:, s] = ax[:, s] + rx[slot, :, s]
                    ay[:, s] = ay[:, s] + ry[slot, :, s]
                    az[s] = az[s] + rz[slot, s]
                hy, hz = (ry, rz) if xi in (0, X - 1) else (ryi, rzi)
                c, nb = near(lambda i: dbuf[slot, s, i], rx.at[slot], hy.at[slot], hz.at[slot], s, xi)
                summed = w_ref[0, xi] * (c - nb[0])
                for j in range(1, 6):
                    summed = summed + w_ref[j, xi] * (c - nb[j])
                xo[s][xi] = xo[s][xi] + c
                res = r_ref[s, xi] - (c + summed)
                r_ref[s, xi] = res
                if not final:
                    nd = a * c + b * res
                    dbuf[nslot, s, xi] = nd
                    put_faces(s, xi, nd)
            if not final:
                for c in outgoing[:5]:
                    c.start()

    def loop_step(k, carry):
        step(k, lax.rem(k, 2), False)
        return carry

    lax.fori_loop(0, CHEB - 1, loop_step, 0)
    step(CHEB - 1, (CHEB - 1) % 2, True)

    for xi in range(X):
        hy, hz = (ay, az) if xi in (0, X - 1) else (ayi, azi)
        c0, n0 = near(lambda i: xo[0][i], ax, hy, hz, 0, xi)
        c1, n1 = near(lambda i: xo[1][i], ax, hy, hz, 1, xi)
        summed = (c0 - n0[0]) * (c1 - n1[0])
        for j in range(1, 6):
            summed = summed + (c0 - n0[j]) * (c1 - n1[j])
        g_ref[xi] = (-0.5 * time_step) * summed


def body(conductivity, stored_state, row_scales, cotangent, upper_bound):
    X, Y, Z = conductivity.shape
    S = 2
    upper = upper_bound[0]
    theta = 0.5 * (upper + 1.0)
    delta = 0.5 * (upper - 1.0)
    sigma = theta / delta
    rho = 1.0 / sigma
    coefs = []
    for _ in range(CHEB):
        rho_next = 1.0 / (2.0 * sigma - rho)
        coefs.append((rho_next * rho, 2.0 * rho_next / delta))
        rho = rho_next
    ab = jnp.stack([
        jnp.stack([c[0] for c in coefs]),
        jnp.stack([c[1] for c in coefs]),
        jnp.broadcast_to(theta, (CHEB,)),
    ])

    ngx = lax.axis_size("gx")
    ngy = lax.axis_size("gy")
    f32 = jnp.float32
    vmem = pl.BlockSpec(memory_space=pltpu.VMEM)
    field = jax.ShapeDtypeStruct((X, Y, Z), f32)
    return pl.pallas_call(
        functools.partial(solve_kernel, ngx, ngy),
        out_shape=(field, field, field, jax.ShapeDtypeStruct((S, X, Y, Z), f32)),
        in_specs=[pl.BlockSpec(memory_space=pltpu.SMEM), vmem, vmem, vmem, vmem],
        out_specs=(vmem, vmem, vmem, vmem),
        scratch_shapes=[
            pltpu.VMEM((6, X, Y, Z), f32),
            pltpu.VMEM((X, Y, Z), stored_state.dtype),
            pltpu.VMEM((2, S, X, Y, Z), f32),
            pltpu.VMEM((2, S, Y, Z), f32),
            pltpu.VMEM((2, S, X, Z), f32),
            pltpu.VMEM((S, 2, X, Y), f32),
            pltpu.VMEM((2, 2, S, Y, Z), f32),
            pltpu.VMEM((2, 2, S, X, Z), f32),
            pltpu.VMEM((2, S, 2, X, Y), f32),
            pltpu.VMEM((2, S, Y, Z), f32),
            pltpu.VMEM((2, S, X, Z), f32),
            pltpu.VMEM((S, 2, X, Y), f32),
            pltpu.VMEM((2, S, X, Z), f32),
            pltpu.VMEM((S, 2, X, Y), f32),
            pltpu.VMEM((2, 2, S, X, Z), f32),
            pltpu.VMEM((2, S, 2, X, Y), f32),
            pltpu.VMEM((2, S, X, Z), f32),
            pltpu.VMEM((S, 2, X, Y), f32),
            pltpu.SemaphoreType.DMA((8, S, 2)),
            pltpu.SemaphoreType.DMA((8, S, 2)),
            pltpu.SemaphoreType.DMA((2,)),
        ],
        compiler_params=pltpu.CompilerParams(
            collective_id=0, has_side_effects=True, vmem_limit_bytes=60 * 1024 * 1024
        ),
    )(ab, conductivity, stored_state, row_scales, cotangent)


def solution(mesh):
    return jax.shard_map(
        body,
        mesh=mesh,
        in_specs=(
            P("gx", "gy", "pa"),
            P("gx", "gy", "pa"),
            P("gx", "gy"),
            P("gx", "gy", "pa"),
            P(),
        ),
        out_specs=(
            P("gx", "gy", "pa"),
            P("gx", "gy", "pa"),
            P("gx", "gy", "pa"),
            P(None, "gx", "gy", "pa"),
        ),
        check_vma=False,
    )
```

```python
import functools

import jax
import jax.numpy as jnp
from jax import lax
from jax.experimental import pallas as pl
from jax.experimental.pallas import tpu as pltpu
from jax.sharding import PartitionSpec as P

CHEB = 16

MESH = pl.DeviceIdType.MESH

time_step = 8.0


def solve_kernel(ngx, ngy, ab_ref, kap_ref, st_ref, rs_ref, cot_ref, g_ref, adj_ref, state_ref, r_ref,
                 w_ref, prev, dbuf, sx, sy, sz, rx, ry, rz, ax, ay, az, send_sem, recv_sem, st_sem):
    S = 2
    X, Y, Z = kap_ref.shape
    xo = (state_ref, adj_ref)
    gx = lax.axis_index("gx")
    gy = lax.axis_index("gy")
    pa = lax.axis_index("pa")
    gx_prev = lax.rem(gx + ngx - 1, ngx)
    gx_next = lax.rem(gx + 1, ngx)
    gy_prev = lax.rem(gy + ngy - 1, ngy)
    gy_next = lax.rem(gy + 1, ngy)
    partner = 1 - pa
    peers = ((gx_prev, gy, pa), (gx_next, gy, pa), (gx, gy_prev, pa), (gx, gy_next, pa), (gx, gy, partner))

    barrier = pltpu.get_barrier_semaphore()
    for dev in peers:
        pl.semaphore_signal(barrier, inc=1, device_id=dev, device_id_type=MESH)
    pl.semaphore_wait(barrier, len(peers))

    def copies(slot, s):
        plan = (
            (sx.at[0, s], rx.at[slot, 1, s], peers[0]),
            (sx.at[1, s], rx.at[slot, 0, s], peers[1]),
            (sy.at[0, s], ry.at[slot, 1, s], peers[2]),
            (sy.at[1, s], ry.at[slot, 0, s], peers[3]),
            (sz.at[s], rz.at[slot, s], peers[4]),
        )
        return [
            pltpu.make_async_remote_copy(
                src_ref=src, dst_ref=dst, send_sem=send_sem.at[i, s, slot], recv_sem=recv_sem.at[i, s, slot],
                device_id=dev, device_id_type=MESH,
            )
            for i, (src, dst, dev) in enumerate(plan)
        ]

    def put_faces(s, xi, plane):
        if xi == 0:
            sx[0, s] = plane
        if xi == X - 1:
            sx[1, s] = plane
        sy[0, s, pl.ds(xi, 1), :] = plane[0:1, :]
        sy[1, s, pl.ds(xi, 1), :] = plane[Y - 1:Y, :]
        t = plane.T
        sz[s, 0, pl.ds(xi, 1), :] = t[0:1, :]
        sz[s, 1, pl.ds(xi, 1), :] = t[Z - 1:Z, :]

    row = lax.broadcasted_iota(jnp.int32, (Y, Z), 0)
    lane = lax.broadcasted_iota(jnp.int32, (Y, Z), 1)

    def near(plane, hx, hy, hz, s, xi):
        c = plane(xi)
        xm = plane(xi - 1) if xi > 0 else hx[0, s]
        xp = plane(xi + 1) if xi < X - 1 else hx[1, s]
        ym = jnp.where(row == 0, jnp.broadcast_to(hy[0, s, pl.ds(xi, 1), :], (Y, Z)), pltpu.roll(c, 1, 0))
        yp = jnp.where(row == Y - 1, jnp.broadcast_to(hy[1, s, pl.ds(xi, 1), :], (Y, Z)),
                       pltpu.roll(c, Y - 1, 0))
        zpair = jnp.where(
            row < Y // 2,
            jnp.broadcast_to(hz[s, 1, pl.ds(xi, 1), :], (Y, Z)),
            jnp.broadcast_to(hz[s, 0, pl.ds(xi, 1), :], (Y, Z)),
        ).T
        zm = jnp.where(lane == 0, zpair, pltpu.roll(c, 1, 1))
        zp = jnp.where(lane == Z - 1, zpair, pltpu.roll(c, Z - 1, 1))
        return c, (xm, xp, ym, yp, zm, zp)

    swap = pltpu.make_async_remote_copy(
        src_ref=st_ref, dst_ref=prev, send_sem=st_sem.at[0], recv_sem=st_sem.at[1],
        device_id=peers[4], device_id_type=MESH,
    )
    swap.start()
    theta = ab_ref[2, 0]

    def start_solve(s):
        for xi in range(X):
            if s == 0:
                scale = jnp.broadcast_to(rs_ref[pl.ds(xi, 1), :], (Z, Y)).T
                rhs = prev[xi].astype(jnp.float32) * scale
            else:
                rhs = cot_ref[xi]
            plane = rhs / theta
            dbuf[0, s, xi] = plane
            xo[s][xi] = jnp.zeros((Y, Z), jnp.float32)
            r_ref[s, xi] = rhs
            put_faces(s, xi, plane)
        for c in copies(0, s):
            c.start()

    start_solve(1)

    for xi in range(X):
        put_faces(0, xi, kap_ref[xi])
    for c in copies(1, 0):
        c.start()
    for c in copies(1, 0):
        c.wait()
    for xi in range(X):
        kc, nb = near(lambda i: kap_ref[i], rx.at[1], ry.at[1], rz.at[1], 0, xi)
        for j in range(6):
            w_ref[j, xi] = (kc + nb[j]) * (0.5 * time_step)

    swap.wait()
    start_solve(0)
    for q in (ax, ay, az):
        q[...] = jnp.zeros(q.shape, jnp.float32)

    def step(k, slot, final):
        nslot = 1 - slot
        a = ab_ref[0, k]
        b = ab_ref[1, k]
        for s in (1, 0):
            incoming = copies(slot, s)
            for c in incoming[2:]:
                c.wait()
            ay[:, s] = ay[:, s] + ry[slot, :, s]
            az[s] = az[s] + rz[slot, s]
            for xi in list(range(1, X - 1)) + [0, X - 1]:
                if xi == 0:
                    for c in incoming[:2]:
                        c.wait()
                    ax[:, s] = ax[:, s] + rx[slot, :, s]
                c, nb = near(lambda i: dbuf[slot, s, i], rx.at[slot], ry.at[slot], rz.at[slot], s, xi)
                summed = w_ref[0, xi] * (c - nb[0])
                for j in range(1, 6):
                    summed = summed + w_ref[j, xi] * (c - nb[j])
                xo[s][xi] = xo[s][xi] + c
                res = r_ref[s, xi] - (c + summed)
                r_ref[s, xi] = res
                if not final:
                    nd = a * c + b * res
                    dbuf[nslot, s, xi] = nd
                    put_faces(s, xi, nd)
            if not final:
                for c in copies(nslot, s):
                    c.start()

    def loop_step(k, carry):
        step(k, lax.rem(k, 2), False)
        return carry

    lax.fori_loop(0, CHEB - 1, loop_step, 0)
    step(CHEB - 1, (CHEB - 1) % 2, True)

    for xi in range(X):
        c0, n0 = near(lambda i: xo[0][i], ax, ay, az, 0, xi)
        c1, n1 = near(lambda i: xo[1][i], ax, ay, az, 1, xi)
        summed = (c0 - n0[0]) * (c1 - n1[0])
        for j in range(1, 6):
            summed = summed + (c0 - n0[j]) * (c1 - n1[j])
        g_ref[xi] = (-0.5 * time_step) * summed


def hand_over(*refs):
    n = len(refs) // 2
    for src, dst in zip(refs[:n], refs[n:]):
        dst[...] = src[...]


def body(conductivity, stored_state, row_scales, cotangent, upper_bound):
    X, Y, Z = conductivity.shape
    S = 2
    upper = upper_bound[0]
    theta = 0.5 * (upper + 1.0)
    delta = 0.5 * (upper - 1.0)
    sigma = theta / delta
    rho = 1.0 / sigma
    coefs = []
    for _ in range(CHEB):
        rho_next = 1.0 / (2.0 * sigma - rho)
        coefs.append((rho_next * rho, 2.0 * rho_next / delta))
        rho = rho_next
    ab = jnp.stack([
        jnp.stack([c[0] for c in coefs]),
        jnp.stack([c[1] for c in coefs]),
        jnp.broadcast_to(theta, (CHEB,)),
    ])

    ngx = lax.axis_size("gx")
    ngy = lax.axis_size("gy")
    f32 = jnp.float32
    vmem = pl.BlockSpec(memory_space=pltpu.VMEM)
    field = jax.ShapeDtypeStruct((X, Y, Z), f32)
    results = pl.pallas_call(
        functools.partial(solve_kernel, ngx, ngy),
        out_shape=(field, field, field, jax.ShapeDtypeStruct((S, X, Y, Z), f32)),
        in_specs=[pl.BlockSpec(memory_space=pltpu.SMEM), vmem, vmem, vmem, vmem],
        out_specs=(vmem, vmem, vmem, vmem),
        scratch_shapes=[
            pltpu.VMEM((6, X, Y, Z), f32),
            pltpu.VMEM((X, Y, Z), stored_state.dtype),
            pltpu.VMEM((2, S, X, Y, Z), f32),
            pltpu.VMEM((2, S, Y, Z), f32),
            pltpu.VMEM((2, S, X, Z), f32),
            pltpu.VMEM((S, 2, X, Y), f32),
            pltpu.VMEM((2, 2, S, Y, Z), f32),
            pltpu.VMEM((2, 2, S, X, Z), f32),
            pltpu.VMEM((2, S, 2, X, Y), f32),
            pltpu.VMEM((2, S, Y, Z), f32),
            pltpu.VMEM((2, S, X, Z), f32),
            pltpu.VMEM((S, 2, X, Y), f32),
            pltpu.SemaphoreType.DMA((5, S, 2)),
            pltpu.SemaphoreType.DMA((5, S, 2)),
            pltpu.SemaphoreType.DMA((2,)),
        ],
        compiler_params=pltpu.CompilerParams(
            collective_id=0, has_side_effects=True, vmem_limit_bytes=60 * 1024 * 1024
        ),
    )(ab, conductivity, stored_state, row_scales, cotangent)
    return pl.pallas_call(
        hand_over,
        out_shape=tuple(jax.ShapeDtypeStruct(o.shape, o.dtype) for o in results),
        in_specs=[vmem] * len(results),
        out_specs=tuple([vmem] * len(results)),
    )(*results)


def solution(mesh):
    return jax.shard_map(
        body,
        mesh=mesh,
        in_specs=(
            P("gx", "gy", "pa"),
            P("gx", "gy", "pa"),
            P("gx", "gy"),
            P("gx", "gy", "pa"),
            P(),
        ),
        out_specs=(
            P("gx", "gy", "pa"),
            P("gx", "gy", "pa"),
            P("gx", "gy", "pa"),
            P(None, "gx", "gy", "pa"),
        ),
        check_vma=False,
    )
```

```python
import functools

import jax
import jax.numpy as jnp
from jax import lax
from jax.experimental import pallas as pl
from jax.experimental.pallas import tpu as pltpu
from jax.sharding import PartitionSpec as P

CHEB = 16

MESH = pl.DeviceIdType.MESH

time_step = 8.0


def solve_kernel(ngx, ngy, ab_ref, kap_ref, st_ref, rs_ref, cot_ref, g_ref, adj_ref, state_ref, r_ref,
                 w_ref, prev, dbuf, sx, sy, sz, rx, ry, rz, ax, ay, az, send_sem, recv_sem, st_sem):
    S = 2
    X, Y, Z = kap_ref.shape
    xo = (state_ref, adj_ref)
    gx = lax.axis_index("gx")
    gy = lax.axis_index("gy")
    pa = lax.axis_index("pa")
    gx_prev = lax.rem(gx + ngx - 1, ngx)
    gx_next = lax.rem(gx + 1, ngx)
    gy_prev = lax.rem(gy + ngy - 1, ngy)
    gy_next = lax.rem(gy + 1, ngy)
    partner = 1 - pa
    peers = ((gx_prev, gy, pa), (gx_next, gy, pa), (gx, gy_prev, pa), (gx, gy_next, pa), (gx, gy, partner))

    barrier = pltpu.get_barrier_semaphore()
    for dev in peers:
        pl.semaphore_signal(barrier, inc=1, device_id=dev, device_id_type=MESH)
    pl.semaphore_wait(barrier, len(peers))

    def copies(slot, s):
        plan = (
            (sx.at[0, s], rx.at[slot, 1, s], peers[0]),
            (sx.at[1, s], rx.at[slot, 0, s], peers[1]),
            (sy.at[0, s], ry.at[slot, 1, s], peers[2]),
            (sy.at[1, s], ry.at[slot, 0, s], peers[3]),
            (sz.at[s], rz.at[slot, s], peers[4]),
        )
        return [
            pltpu.make_async_remote_copy(
                src_ref=src, dst_ref=dst, send_sem=send_sem.at[i, s, slot], recv_sem=recv_sem.at[i, s, slot],
                device_id=dev, device_id_type=MESH,
            )
            for i, (src, dst, dev) in enumerate(plan)
        ]

    def put_faces(s, xi, plane):
        if xi == 0:
            sx[0, s] = plane
        if xi == X - 1:
            sx[1, s] = plane
        sy[0, s, pl.ds(xi, 1), :] = plane[0:1, :]
        sy[1, s, pl.ds(xi, 1), :] = plane[Y - 1:Y, :]
        t = plane.T
        sz[s, 0, pl.ds(xi, 1), :] = t[0:1, :]
        sz[s, 1, pl.ds(xi, 1), :] = t[Z - 1:Z, :]

    row = lax.broadcasted_iota(jnp.int32, (Y, Z), 0)
    lane = lax.broadcasted_iota(jnp.int32, (Y, Z), 1)

    def near(plane, hx, hy, hz, s, xi):
        c = plane(xi)
        xm = plane(xi - 1) if xi > 0 else hx[0, s]
        xp = plane(xi + 1) if xi < X - 1 else hx[1, s]
        ym = jnp.where(row == 0, jnp.broadcast_to(hy[0, s, pl.ds(xi, 1), :], (Y, Z)), pltpu.roll(c, 1, 0))
        yp = jnp.where(row == Y - 1, jnp.broadcast_to(hy[1, s, pl.ds(xi, 1), :], (Y, Z)),
                       pltpu.roll(c, Y - 1, 0))
        zpair = jnp.where(
            row < Y // 2,
            jnp.broadcast_to(hz[s, 1, pl.ds(xi, 1), :], (Y, Z)),
            jnp.broadcast_to(hz[s, 0, pl.ds(xi, 1), :], (Y, Z)),
        ).T
        zm = jnp.where(lane == 0, zpair, pltpu.roll(c, 1, 1))
        zp = jnp.where(lane == Z - 1, zpair, pltpu.roll(c, Z - 1, 1))
        return c, (xm, xp, ym, yp, zm, zp)

    swap = pltpu.make_async_remote_copy(
        src_ref=st_ref, dst_ref=prev, send_sem=st_sem.at[0], recv_sem=st_sem.at[1],
        device_id=peers[4], device_id_type=MESH,
    )
    swap.start()
    theta = ab_ref[2, 0]

    def start_solve(s):
        for xi in range(X):
            if s == 0:
                scale = jnp.broadcast_to(rs_ref[pl.ds(xi, 1), :], (Z, Y)).T
                rhs = prev[xi].astype(jnp.float32) * scale
            else:
                rhs = cot_ref[xi]
            plane = rhs / theta
            dbuf[0, s, xi] = plane
            xo[s][xi] = jnp.zeros((Y, Z), jnp.float32)
            r_ref[s, xi] = rhs
            put_faces(s, xi, plane)
        for c in copies(0, s):
            c.start()

    start_solve(1)

    for xi in range(X):
        put_faces(0, xi, kap_ref[xi])
    for c in copies(1, 0):
        c.start()
    for c in copies(1, 0):
        c.wait()
    for xi in range(X):
        kc, nb = near(lambda i: kap_ref[i], rx.at[1], ry.at[1], rz.at[1], 0, xi)
        for j in range(6):
            w_ref[j, xi] = (kc + nb[j]) * (0.5 * time_step)

    swap.wait()
    start_solve(0)
    for q in (ax, ay, az):
        q[...] = jnp.zeros(q.shape, jnp.float32)

    def step(k, slot, final):
        nslot = 1 - slot
        a = ab_ref[0, k]
        b = ab_ref[1, k]
        for s in (1, 0):
            incoming = copies(slot, s)
            for c in incoming[2:]:
                c.wait()
            ay[:, s] = ay[:, s] + ry[slot, :, s]
            az[s] = az[s] + rz[slot, s]
            for xi in list(range(1, X - 1)) + [0, X - 1]:
                if xi == 0:
                    for c in incoming[:2]:
                        c.wait()
                    ax[:, s] = ax[:, s] + rx[slot, :, s]
                c, nb = near(lambda i: dbuf[slot, s, i], rx.at[slot], ry.at[slot], rz.at[slot], s, xi)
                summed = w_ref[0, xi] * (c - nb[0])
                for j in range(1, 6):
                    summed = summed + w_ref[j, xi] * (c - nb[j])
                xo[s][xi] = xo[s][xi] + c
                res = r_ref[s, xi] - (c + summed)
                r_ref[s, xi] = res
                if not final:
                    nd = a * c + b * res
                    dbuf[nslot, s, xi] = nd
                    put_faces(s, xi, nd)
            if not final:
                for c in copies(nslot, s):
                    c.start()

    def loop_step(k, carry):
        step(k, lax.rem(k, 2), False)
        return carry

    lax.fori_loop(0, CHEB - 1, loop_step, 0)
    step(CHEB - 1, (CHEB - 1) % 2, True)

    for xi in range(X):
        c0, n0 = near(lambda i: xo[0][i], ax, ay, az, 0, xi)
        c1, n1 = near(lambda i: xo[1][i], ax, ay, az, 1, xi)
        summed = (c0 - n0[0]) * (c1 - n1[0])
        for j in range(1, 6):
            summed = summed + (c0 - n0[j]) * (c1 - n1[j])
        g_ref[xi] = (-0.5 * time_step) * summed


def hand_over(*refs):
    n = len(refs) // 2
    for src, dst in zip(refs[:n], refs[n:]):
        dst[...] = src[...]


def body(conductivity, stored_state, row_scales, cotangent, upper_bound):
    X, Y, Z = conductivity.shape
    S = 2
    upper = upper_bound[0]
    theta = 0.5 * (upper + 1.0)
    delta = 0.5 * (upper - 1.0)
    sigma = theta / delta
    rho = 1.0 / sigma
    coefs = []
    for _ in range(CHEB):
        rho_next = 1.0 / (2.0 * sigma - rho)
        coefs.append((rho_next * rho, 2.0 * rho_next / delta))
        rho = rho_next
    ab = jnp.stack([
        jnp.stack([c[0] for c in coefs]),
        jnp.stack([c[1] for c in coefs]),
        jnp.broadcast_to(theta, (CHEB,)),
    ])

    ngx = lax.axis_size("gx")
    ngy = lax.axis_size("gy")
    f32 = jnp.float32
    vmem = pl.BlockSpec(memory_space=pltpu.VMEM)
    field = jax.ShapeDtypeStruct((X, Y, Z), f32)
    results = pl.pallas_call(
        functools.partial(solve_kernel, ngx, ngy),
        out_shape=(field, field, field, jax.ShapeDtypeStruct((S, X, Y, Z), f32)),
        in_specs=[pl.BlockSpec(memory_space=pltpu.SMEM), vmem, vmem, vmem, vmem],
        out_specs=(vmem, vmem, vmem, vmem),
        scratch_shapes=[
            pltpu.VMEM((6, X, Y, Z), f32),
            pltpu.VMEM((X, Y, Z), stored_state.dtype),
            pltpu.VMEM((2, S, X, Y, Z), f32),
            pltpu.VMEM((2, S, Y, Z), f32),
            pltpu.VMEM((2, S, X, Z), f32),
            pltpu.VMEM((S, 2, X, Y), f32),
            pltpu.VMEM((2, 2, S, Y, Z), f32),
            pltpu.VMEM((2, 2, S, X, Z), f32),
            pltpu.VMEM((2, S, 2, X, Y), f32),
            pltpu.VMEM((2, S, Y, Z), f32),
            pltpu.VMEM((2, S, X, Z), f32),
            pltpu.VMEM((S, 2, X, Y), f32),
            pltpu.SemaphoreType.DMA((5, S, 2)),
            pltpu.SemaphoreType.DMA((5, S, 2)),
            pltpu.SemaphoreType.DMA((2,)),
        ],
        compiler_params=pltpu.CompilerParams(
            collective_id=0, has_side_effects=True, vmem_limit_bytes=60 * 1024 * 1024
        ),
    )(ab, conductivity, stored_state, row_scales, cotangent)
    planes = 2
    specs = [
        pl.BlockSpec((planes, Y, Z), lambda i: (i, 0, 0)) if o.ndim == 3
        else pl.BlockSpec((S, planes, Y, Z), lambda i: (0, i, 0, 0))
        for o in results
    ]
    return pl.pallas_call(
        hand_over,
        grid=(X // planes,),
        out_shape=tuple(jax.ShapeDtypeStruct(o.shape, o.dtype) for o in results),
        in_specs=specs,
        out_specs=tuple(specs),
    )(*results)


def solution(mesh):
    return jax.shard_map(
        body,
        mesh=mesh,
        in_specs=(
            P("gx", "gy", "pa"),
            P("gx", "gy", "pa"),
            P("gx", "gy"),
            P("gx", "gy", "pa"),
            P(),
        ),
        out_specs=(
            P("gx", "gy", "pa"),
            P("gx", "gy", "pa"),
            P("gx", "gy", "pa"),
            P(None, "gx", "gy", "pa"),
        ),
        check_vma=False,
    )
```

```python
import functools

import jax
import jax.numpy as jnp
from jax import lax
from jax.experimental import pallas as pl
from jax.experimental.pallas import tpu as pltpu
from jax.sharding import PartitionSpec as P

CHEB = 16

MESH = pl.DeviceIdType.MESH

time_step = 8.0


def solve_kernel(ngx, ngy, ub_ref, kap_ref, st_ref, rs_ref, cot_ref, g_ref, adj_ref, state_ref, r_ref,
                 w_ref, prev, dbuf, sx, sy, sz, rx, ry, rz, ax, ay, az, coef, send_sem, recv_sem, st_sem):
    S = 2
    X, Y, Z = kap_ref.shape
    xo = (state_ref, adj_ref)
    gx = lax.axis_index("gx")
    gy = lax.axis_index("gy")
    pa = lax.axis_index("pa")
    gx_prev = lax.rem(gx + ngx - 1, ngx)
    gx_next = lax.rem(gx + 1, ngx)
    gy_prev = lax.rem(gy + ngy - 1, ngy)
    gy_next = lax.rem(gy + 1, ngy)
    partner = 1 - pa
    peers = ((gx_prev, gy, pa), (gx_next, gy, pa), (gx, gy_prev, pa), (gx, gy_next, pa), (gx, gy, partner))

    barrier = pltpu.get_barrier_semaphore()
    for dev in peers:
        pl.semaphore_signal(barrier, inc=1, device_id=dev, device_id_type=MESH)
    pl.semaphore_wait(barrier, len(peers))

    def copies(slot, s):
        plan = (
            (sx.at[0, s], rx.at[slot, 1, s], peers[0]),
            (sx.at[1, s], rx.at[slot, 0, s], peers[1]),
            (sy.at[0, s], ry.at[slot, 1, s], peers[2]),
            (sy.at[1, s], ry.at[slot, 0, s], peers[3]),
            (sz.at[s], rz.at[slot, s], peers[4]),
        )
        return [
            pltpu.make_async_remote_copy(
                src_ref=src, dst_ref=dst, send_sem=send_sem.at[i, s, slot], recv_sem=recv_sem.at[i, s, slot],
                device_id=dev, device_id_type=MESH,
            )
            for i, (src, dst, dev) in enumerate(plan)
        ]

    def put_faces(s, xi, plane):
        if xi == 0:
            sx[0, s] = plane
        if xi == X - 1:
            sx[1, s] = plane
        sy[0, s, pl.ds(xi, 1), :] = plane[0:1, :]
        sy[1, s, pl.ds(xi, 1), :] = plane[Y - 1:Y, :]
        t = plane.T
        sz[s, 0, pl.ds(xi, 1), :] = t[0:1, :]
        sz[s, 1, pl.ds(xi, 1), :] = t[Z - 1:Z, :]

    row = lax.broadcasted_iota(jnp.int32, (Y, Z), 0)
    lane = lax.broadcasted_iota(jnp.int32, (Y, Z), 1)

    def near(plane, hx, hy, hz, s, xi):
        c = plane(xi)
        xm = plane(xi - 1) if xi > 0 else hx[0, s]
        xp = plane(xi + 1) if xi < X - 1 else hx[1, s]
        ym = jnp.where(row == 0, jnp.broadcast_to(hy[0, s, pl.ds(xi, 1), :], (Y, Z)), pltpu.roll(c, 1, 0))
        yp = jnp.where(row == Y - 1, jnp.broadcast_to(hy[1, s, pl.ds(xi, 1), :], (Y, Z)),
                       pltpu.roll(c, Y - 1, 0))
        zpair = jnp.where(
            row < Y // 2,
            jnp.broadcast_to(hz[s, 1, pl.ds(xi, 1), :], (Y, Z)),
            jnp.broadcast_to(hz[s, 0, pl.ds(xi, 1), :], (Y, Z)),
        ).T
        zm = jnp.where(lane == 0, zpair, pltpu.roll(c, 1, 1))
        zp = jnp.where(lane == Z - 1, zpair, pltpu.roll(c, Z - 1, 1))
        return c, (xm, xp, ym, yp, zm, zp)

    swap = pltpu.make_async_remote_copy(
        src_ref=st_ref, dst_ref=prev, send_sem=st_sem.at[0], recv_sem=st_sem.at[1],
        device_id=peers[4], device_id_type=MESH,
    )
    swap.start()
    upper = jnp.full((8, Z), ub_ref[0], jnp.float32)
    theta_v = 0.5 * (upper + 1.0)
    delta = 0.5 * (upper - 1.0)
    sigma = theta_v / delta
    rho = 1.0 / sigma
    for k in range(CHEB):
        rho_next = 1.0 / (2.0 * sigma - rho)
        coef[0, k] = rho_next * rho
        coef[1, k] = 2.0 * rho_next / delta
        rho = rho_next
    theta = jnp.broadcast_to(theta_v[0:1, :], (Y, Z))

    def start_solve(s):
        for xi in range(X):
            if s == 0:
                scale = jnp.broadcast_to(rs_ref[pl.ds(xi, 1), :], (Z, Y)).T
                rhs = prev[xi].astype(jnp.float32) * scale
            else:
                rhs = cot_ref[xi]
            plane = rhs / theta
            dbuf[0, s, xi] = plane
            xo[s][xi] = jnp.zeros((Y, Z), jnp.float32)
            r_ref[s, xi] = rhs
            put_faces(s, xi, plane)
        for c in copies(0, s):
            c.start()

    start_solve(1)

    for xi in range(X):
        put_faces(0, xi, kap_ref[xi])
    for c in copies(1, 0):
        c.start()
    for c in copies(1, 0):
        c.wait()
    for xi in range(X):
        kc, nb = near(lambda i: kap_ref[i], rx.at[1], ry.at[1], rz.at[1], 0, xi)
        for j in range(6):
            w_ref[j, xi] = (kc + nb[j]) * (0.5 * time_step)

    swap.wait()
    start_solve(0)
    for q in (ax, ay, az):
        q[...] = jnp.zeros(q.shape, jnp.float32)

    def step(k, slot, final):
        nslot = 1 - slot
        a = jnp.broadcast_to(coef[0, k, 0:1, :], (Y, Z))
        b = jnp.broadcast_to(coef[1, k, 0:1, :], (Y, Z))
        for s in (1, 0):
            incoming = copies(slot, s)
            for c in incoming[2:]:
                c.wait()
            ay[:, s] = ay[:, s] + ry[slot, :, s]
            az[s] = az[s] + rz[slot, s]
            for xi in list(range(1, X - 1)) + [0, X - 1]:
                if xi == 0:
                    for c in incoming[:2]:
                        c.wait()
                    ax[:, s] = ax[:, s] + rx[slot, :, s]
                c, nb = near(lambda i: dbuf[slot, s, i], rx.at[slot], ry.at[slot], rz.at[slot], s, xi)
                summed = w_ref[0, xi] * (c - nb[0])
                for j in range(1, 6):
                    summed = summed + w_ref[j, xi] * (c - nb[j])
                xo[s][xi] = xo[s][xi] + c
                res = r_ref[s, xi] - (c + summed)
                r_ref[s, xi] = res
                if not final:
                    nd = a * c + b * res
                    dbuf[nslot, s, xi] = nd
                    put_faces(s, xi, nd)
            if not final:
                for c in copies(nslot, s):
                    c.start()

    def loop_step(k, carry):
        step(k, lax.rem(k, 2), False)
        return carry

    lax.fori_loop(0, CHEB - 1, loop_step, 0)
    step(CHEB - 1, (CHEB - 1) % 2, True)

    for xi in range(X):
        c0, n0 = near(lambda i: xo[0][i], ax, ay, az, 0, xi)
        c1, n1 = near(lambda i: xo[1][i], ax, ay, az, 1, xi)
        summed = (c0 - n0[0]) * (c1 - n1[0])
        for j in range(1, 6):
            summed = summed + (c0 - n0[j]) * (c1 - n1[j])
        g_ref[xi] = (-0.5 * time_step) * summed


def hand_over(*refs):
    n = len(refs) // 2
    for src, dst in zip(refs[:n], refs[n:]):
        dst[...] = src[...]


def body(conductivity, stored_state, row_scales, cotangent, upper_bound):
    X, Y, Z = conductivity.shape
    S = 2
    ngx = lax.axis_size("gx")
    ngy = lax.axis_size("gy")
    f32 = jnp.float32
    vmem = pl.BlockSpec(memory_space=pltpu.VMEM)
    field = jax.ShapeDtypeStruct((X, Y, Z), f32)
    results = pl.pallas_call(
        functools.partial(solve_kernel, ngx, ngy),
        out_shape=(field, field, field, jax.ShapeDtypeStruct((S, X, Y, Z), f32)),
        in_specs=[pl.BlockSpec(memory_space=pltpu.SMEM), vmem, vmem, vmem, vmem],
        out_specs=(vmem, vmem, vmem, vmem),
        scratch_shapes=[
            pltpu.VMEM((6, X, Y, Z), f32),
            pltpu.VMEM((X, Y, Z), stored_state.dtype),
            pltpu.VMEM((2, S, X, Y, Z), f32),
            pltpu.VMEM((2, S, Y, Z), f32),
            pltpu.VMEM((2, S, X, Z), f32),
            pltpu.VMEM((S, 2, X, Y), f32),
            pltpu.VMEM((2, 2, S, Y, Z), f32),
            pltpu.VMEM((2, 2, S, X, Z), f32),
            pltpu.VMEM((2, S, 2, X, Y), f32),
            pltpu.VMEM((2, S, Y, Z), f32),
            pltpu.VMEM((2, S, X, Z), f32),
            pltpu.VMEM((S, 2, X, Y), f32),
            pltpu.VMEM((2, CHEB, 8, Z), f32),
            pltpu.SemaphoreType.DMA((5, S, 2)),
            pltpu.SemaphoreType.DMA((5, S, 2)),
            pltpu.SemaphoreType.DMA((2,)),
        ],
        compiler_params=pltpu.CompilerParams(
            collective_id=0, has_side_effects=True, vmem_limit_bytes=60 * 1024 * 1024
        ),
    )(upper_bound, conductivity, stored_state, row_scales, cotangent)
    return pl.pallas_call(
        hand_over,
        out_shape=tuple(jax.ShapeDtypeStruct(o.shape, o.dtype) for o in results),
        in_specs=[vmem] * len(results),
        out_specs=tuple([vmem] * len(results)),
    )(*results)


def solution(mesh):
    return jax.shard_map(
        body,
        mesh=mesh,
        in_specs=(
            P("gx", "gy", "pa"),
            P("gx", "gy", "pa"),
            P("gx", "gy"),
            P("gx", "gy", "pa"),
            P(),
        ),
        out_specs=(
            P("gx", "gy", "pa"),
            P("gx", "gy", "pa"),
            P("gx", "gy", "pa"),
            P(None, "gx", "gy", "pa"),
        ),
        check_vma=False,
    )
```

```python
import functools

import jax
import jax.numpy as jnp
from jax import lax
from jax.experimental import pallas as pl
from jax.experimental.pallas import tpu as pltpu
from jax.sharding import PartitionSpec as P

CHEB = 16

MESH = pl.DeviceIdType.MESH

time_step = 8.0


def solve_kernel(ngx, ngy, ub_ref, kap_ref, st_ref, rs_ref, cot_ref, g_ref, adj_ref, state_ref, r_ref,
                 w_ref, prev, dbuf, sx, sy, sz, rx, ry, rz, ax, ay, az, coef, send_sem, recv_sem, st_sem):
    S = 2
    X, Y, Z = kap_ref.shape
    xo = (state_ref, adj_ref)
    gx = lax.axis_index("gx")
    gy = lax.axis_index("gy")
    pa = lax.axis_index("pa")
    gx_prev = lax.rem(gx + ngx - 1, ngx)
    gx_next = lax.rem(gx + 1, ngx)
    gy_prev = lax.rem(gy + ngy - 1, ngy)
    gy_next = lax.rem(gy + 1, ngy)
    partner = 1 - pa
    peers = ((gx_prev, gy, pa), (gx_next, gy, pa), (gx, gy_prev, pa), (gx, gy_next, pa), (gx, gy, partner))

    barrier = pltpu.get_barrier_semaphore()
    for dev in peers:
        pl.semaphore_signal(barrier, inc=1, device_id=dev, device_id_type=MESH)
    pl.semaphore_wait(barrier, len(peers))

    def copies(slot, s):
        plan = (
            (sx.at[0, s], rx.at[slot, 1, s], peers[0]),
            (sx.at[1, s], rx.at[slot, 0, s], peers[1]),
            (sy.at[0, s], ry.at[slot, 1, s], peers[2]),
            (sy.at[1, s], ry.at[slot, 0, s], peers[3]),
            (sz.at[s], rz.at[slot, s], peers[4]),
        )
        return [
            pltpu.make_async_remote_copy(
                src_ref=src, dst_ref=dst, send_sem=send_sem.at[i, s, slot], recv_sem=recv_sem.at[i, s, slot],
                device_id=dev, device_id_type=MESH,
            )
            for i, (src, dst, dev) in enumerate(plan)
        ]

    def put_faces(s, xi, plane):
        if xi == 0:
            sx[0, s] = plane
        if xi == X - 1:
            sx[1, s] = plane
        sy[0, s, pl.ds(xi, 1), :] = plane[0:1, :]
        sy[1, s, pl.ds(xi, 1), :] = plane[Y - 1:Y, :]
        t = plane.T
        sz[s, 0, pl.ds(xi, 1), :] = t[0:1, :]
        sz[s, 1, pl.ds(xi, 1), :] = t[Z - 1:Z, :]

    row = lax.broadcasted_iota(jnp.int32, (Y, Z), 0)
    lane = lax.broadcasted_iota(jnp.int32, (Y, Z), 1)

    def near(plane, hx, hy, hz, s, xi):
        c = plane(xi)
        xm = plane(xi - 1) if xi > 0 else hx[0, s]
        xp = plane(xi + 1) if xi < X - 1 else hx[1, s]
        ym = jnp.where(row == 0, jnp.broadcast_to(hy[0, s, pl.ds(xi, 1), :], (Y, Z)), pltpu.roll(c, 1, 0))
        yp = jnp.where(row == Y - 1, jnp.broadcast_to(hy[1, s, pl.ds(xi, 1), :], (Y, Z)),
                       pltpu.roll(c, Y - 1, 0))
        zpair = jnp.where(
            row < Y // 2,
            jnp.broadcast_to(hz[s, 1, pl.ds(xi, 1), :], (Y, Z)),
            jnp.broadcast_to(hz[s, 0, pl.ds(xi, 1), :], (Y, Z)),
        ).T
        zm = jnp.where(lane == 0, zpair, pltpu.roll(c, 1, 1))
        zp = jnp.where(lane == Z - 1, zpair, pltpu.roll(c, Z - 1, 1))
        return c, (xm, xp, ym, yp, zm, zp)

    swap = pltpu.make_async_remote_copy(
        src_ref=st_ref, dst_ref=prev, send_sem=st_sem.at[0], recv_sem=st_sem.at[1],
        device_id=peers[4], device_id_type=MESH,
    )
    swap.start()
    upper = jnp.full((8, Z), ub_ref[0], jnp.float32)
    theta_v = 0.5 * (upper + 1.0)
    delta = 0.5 * (upper - 1.0)
    sigma = theta_v / delta
    rho = 1.0 / sigma
    for k in range(CHEB):
        rho_next = 1.0 / (2.0 * sigma - rho)
        coef[0, k] = rho_next * rho
        coef[1, k] = 2.0 * rho_next / delta
        rho = rho_next
    theta = jnp.broadcast_to(theta_v[0:1, :], (Y, Z))

    def start_solve(s):
        for xi in range(X):
            if s == 0:
                scale = jnp.broadcast_to(rs_ref[pl.ds(xi, 1), :], (Z, Y)).T
                rhs = prev[xi].astype(jnp.float32) * scale
            else:
                rhs = cot_ref[xi]
            plane = rhs / theta
            dbuf[0, s, xi] = plane
            xo[s][xi] = jnp.zeros((Y, Z), jnp.float32)
            r_ref[s, xi] = rhs
            put_faces(s, xi, plane)
        for c in copies(0, s):
            c.start()

    start_solve(1)

    for xi in range(X):
        put_faces(0, xi, kap_ref[xi])
    for c in copies(1, 0):
        c.start()
    for c in copies(1, 0):
        c.wait()
    for xi in range(X):
        kc, nb = near(lambda i: kap_ref[i], rx.at[1], ry.at[1], rz.at[1], 0, xi)
        for j in range(6):
            w_ref[j, xi] = (kc + nb[j]) * (0.5 * time_step)

    swap.wait()
    start_solve(0)
    for q in (ax, ay, az):
        q[...] = jnp.zeros(q.shape, jnp.float32)

    def step(k, slot, final):
        nslot = 1 - slot
        a = jnp.broadcast_to(coef[0, k, 0:1, :], (Y, Z))
        b = jnp.broadcast_to(coef[1, k, 0:1, :], (Y, Z))
        for s in (1, 0):
            incoming = copies(slot, s)
            for c in incoming[2:]:
                c.wait()
            ay[:, s] = ay[:, s] + ry[slot, :, s]
            az[s] = az[s] + rz[slot, s]
            for xi in list(range(1, X - 1)) + [0, X - 1]:
                if xi == 0:
                    for c in incoming[:2]:
                        c.wait()
                    ax[:, s] = ax[:, s] + rx[slot, :, s]
                c, nb = near(lambda i: dbuf[slot, s, i], rx.at[slot], ry.at[slot], rz.at[slot], s, xi)
                summed = w_ref[0, xi] * (c - nb[0])
                for j in range(1, 6):
                    summed = summed + w_ref[j, xi] * (c - nb[j])
                xo[s][xi] = xo[s][xi] + c
                res = r_ref[s, xi] - (c + summed)
                r_ref[s, xi] = res
                if not final:
                    nd = a * c + b * res
                    dbuf[nslot, s, xi] = nd
                    put_faces(s, xi, nd)
            if not final:
                for c in copies(nslot, s):
                    c.start()

    def loop_step(k, carry):
        step(k, lax.rem(k, 2), False)
        return carry

    lax.fori_loop(0, CHEB - 1, loop_step, 0)
    step(CHEB - 1, (CHEB - 1) % 2, True)

    for xi in range(X):
        c0, n0 = near(lambda i: xo[0][i], ax, ay, az, 0, xi)
        c1, n1 = near(lambda i: xo[1][i], ax, ay, az, 1, xi)
        summed = (c0 - n0[0]) * (c1 - n1[0])
        for j in range(1, 6):
            summed = summed + (c0 - n0[j]) * (c1 - n1[j])
        g_ref[xi] = (-0.5 * time_step) * summed


def hand_over(*refs):
    n = (len(refs) - 1) // 2
    srcs, dsts, sem = refs[:n], refs[n:2 * n], refs[2 * n]
    moves = [pltpu.make_async_copy(src, dst, sem.at[i]) for i, (src, dst) in enumerate(zip(srcs, dsts))]
    for m in moves:
        m.start()
    for m in moves:
        m.wait()


def body(conductivity, stored_state, row_scales, cotangent, upper_bound):
    X, Y, Z = conductivity.shape
    S = 2
    ngx = lax.axis_size("gx")
    ngy = lax.axis_size("gy")
    f32 = jnp.float32
    vmem = pl.BlockSpec(memory_space=pltpu.VMEM)
    field = jax.ShapeDtypeStruct((X, Y, Z), f32)
    results = pl.pallas_call(
        functools.partial(solve_kernel, ngx, ngy),
        out_shape=(field, field, field, jax.ShapeDtypeStruct((S, X, Y, Z), f32)),
        in_specs=[pl.BlockSpec(memory_space=pltpu.SMEM), vmem, vmem, vmem, vmem],
        out_specs=(vmem, vmem, vmem, vmem),
        scratch_shapes=[
            pltpu.VMEM((6, X, Y, Z), f32),
            pltpu.VMEM((X, Y, Z), stored_state.dtype),
            pltpu.VMEM((2, S, X, Y, Z), f32),
            pltpu.VMEM((2, S, Y, Z), f32),
            pltpu.VMEM((2, S, X, Z), f32),
            pltpu.VMEM((S, 2, X, Y), f32),
            pltpu.VMEM((2, 2, S, Y, Z), f32),
            pltpu.VMEM((2, 2, S, X, Z), f32),
            pltpu.VMEM((2, S, 2, X, Y), f32),
            pltpu.VMEM((2, S, Y, Z), f32),
            pltpu.VMEM((2, S, X, Z), f32),
            pltpu.VMEM((S, 2, X, Y), f32),
            pltpu.VMEM((2, CHEB, 8, Z), f32),
            pltpu.SemaphoreType.DMA((5, S, 2)),
            pltpu.SemaphoreType.DMA((5, S, 2)),
            pltpu.SemaphoreType.DMA((2,)),
        ],
        compiler_params=pltpu.CompilerParams(
            collective_id=0, has_side_effects=True, vmem_limit_bytes=60 * 1024 * 1024
        ),
    )(upper_bound, conductivity, stored_state, row_scales, cotangent)
    return pl.pallas_call(
        hand_over,
        out_shape=tuple(jax.ShapeDtypeStruct(o.shape, o.dtype) for o in results),
        in_specs=[pl.BlockSpec(memory_space=pl.ANY)] * len(results),
        out_specs=tuple([vmem] * len(results)),
        scratch_shapes=[pltpu.SemaphoreType.DMA((len(results),))],
    )(*results)


def solution(mesh):
    return jax.shard_map(
        body,
        mesh=mesh,
        in_specs=(
            P("gx", "gy", "pa"),
            P("gx", "gy", "pa"),
            P("gx", "gy"),
            P("gx", "gy", "pa"),
            P(),
        ),
        out_specs=(
            P("gx", "gy", "pa"),
            P("gx", "gy", "pa"),
            P("gx", "gy", "pa"),
            P(None, "gx", "gy", "pa"),
        ),
        check_vma=False,
    )
```

```python
import functools

import jax
import jax.numpy as jnp
from jax import lax
from jax.experimental import pallas as pl
from jax.experimental.pallas import tpu as pltpu
from jax.sharding import PartitionSpec as P

CHEB = 16

MESH = pl.DeviceIdType.MESH

time_step = 8.0


def solve_kernel(ngx, ngy, ub_ref, kap_ref, st_ref, rs_ref, cot_ref, g_ref, adj_ref, state_ref, r_ref,
                 w_ref, prev, dbuf, sx, sy, sz, rx, ry, rz, ax, ay, az, coef, send_sem, recv_sem, st_sem):
    S = 2
    X, Y, Z = kap_ref.shape
    xo = (state_ref, adj_ref)
    gx = lax.axis_index("gx")
    gy = lax.axis_index("gy")
    pa = lax.axis_index("pa")
    gx_prev = lax.rem(gx + ngx - 1, ngx)
    gx_next = lax.rem(gx + 1, ngx)
    gy_prev = lax.rem(gy + ngy - 1, ngy)
    gy_next = lax.rem(gy + 1, ngy)
    partner = 1 - pa
    peers = ((gx_prev, gy, pa), (gx_next, gy, pa), (gx, gy_prev, pa), (gx, gy_next, pa), (gx, gy, partner))

    barrier = pltpu.get_barrier_semaphore()
    for dev in peers:
        pl.semaphore_signal(barrier, inc=1, device_id=dev, device_id_type=MESH)
    pl.semaphore_wait(barrier, len(peers))

    def copies(slot, s):
        plan = (
            (sx.at[0, s], rx.at[slot, 1, s], peers[0]),
            (sx.at[1, s], rx.at[slot, 0, s], peers[1]),
            (sy.at[0, s], ry.at[slot, 1, s], peers[2]),
            (sy.at[1, s], ry.at[slot, 0, s], peers[3]),
            (sz.at[s], rz.at[slot, s], peers[4]),
        )
        return [
            pltpu.make_async_remote_copy(
                src_ref=src, dst_ref=dst, send_sem=send_sem.at[i, s, slot], recv_sem=recv_sem.at[i, s, slot],
                device_id=dev, device_id_type=MESH,
            )
            for i, (src, dst, dev) in enumerate(plan)
        ]

    def put_faces(s, xi, plane):
        if xi == 0:
            sx[0, s] = plane
        if xi == X - 1:
            sx[1, s] = plane
        sy[0, s, pl.ds(xi, 1), :] = plane[0:1, :]
        sy[1, s, pl.ds(xi, 1), :] = plane[Y - 1:Y, :]
        t = plane.T
        sz[s, 0, pl.ds(xi, 1), :] = t[0:1, :]
        sz[s, 1, pl.ds(xi, 1), :] = t[Z - 1:Z, :]

    row = lax.broadcasted_iota(jnp.int32, (Y, Z), 0)
    lane = lax.broadcasted_iota(jnp.int32, (Y, Z), 1)

    def near(plane, hx, hy, hz, s, xi):
        c = plane(xi)
        xm = plane(xi - 1) if xi > 0 else hx[0, s]
        xp = plane(xi + 1) if xi < X - 1 else hx[1, s]
        ym = jnp.where(row == 0, jnp.broadcast_to(hy[0, s, pl.ds(xi, 1), :], (Y, Z)), pltpu.roll(c, 1, 0))
        yp = jnp.where(row == Y - 1, jnp.broadcast_to(hy[1, s, pl.ds(xi, 1), :], (Y, Z)),
                       pltpu.roll(c, Y - 1, 0))
        zpair = jnp.where(
            row < Y // 2,
            jnp.broadcast_to(hz[s, 1, pl.ds(xi, 1), :], (Y, Z)),
            jnp.broadcast_to(hz[s, 0, pl.ds(xi, 1), :], (Y, Z)),
        ).T
        zm = jnp.where(lane == 0, zpair, pltpu.roll(c, 1, 1))
        zp = jnp.where(lane == Z - 1, zpair, pltpu.roll(c, Z - 1, 1))
        return c, (xm, xp, ym, yp, zm, zp)

    swap = pltpu.make_async_remote_copy(
        src_ref=st_ref, dst_ref=prev, send_sem=st_sem.at[0], recv_sem=st_sem.at[1],
        device_id=peers[4], device_id_type=MESH,
    )
    swap.start()
    upper = jnp.full((8, Z), ub_ref[0], jnp.float32)
    theta_v = 0.5 * (upper + 1.0)
    delta = 0.5 * (upper - 1.0)
    sigma = theta_v / delta
    rho = 1.0 / sigma
    for k in range(CHEB):
        rho_next = 1.0 / (2.0 * sigma - rho)
        coef[0, k] = rho_next * rho
        coef[1, k] = 2.0 * rho_next / delta
        rho = rho_next
    theta = jnp.broadcast_to(theta_v[0:1, :], (Y, Z))

    def start_solve(s):
        for xi in range(X):
            if s == 0:
                scale = jnp.broadcast_to(rs_ref[pl.ds(xi, 1), :], (Z, Y)).T
                rhs = prev[xi].astype(jnp.float32) * scale
            else:
                rhs = cot_ref[xi]
            plane = rhs / theta
            dbuf[0, s, xi] = plane
            xo[s][xi] = jnp.zeros((Y, Z), jnp.float32)
            r_ref[s, xi] = rhs
            put_faces(s, xi, plane)
        for c in copies(0, s):
            c.start()

    for xi in range(X):
        put_faces(0, xi, kap_ref[xi])
    for c in copies(1, 0):
        c.start()

    start_solve(1)

    for c in copies(1, 0):
        c.wait()
    for xi in range(X):
        kc, nb = near(lambda i: kap_ref[i], rx.at[1], ry.at[1], rz.at[1], 0, xi)
        for j in range(6):
            w_ref[j, xi] = (kc + nb[j]) * (0.5 * time_step)

    swap.wait()
    start_solve(0)
    for q in (ax, ay, az):
        q[...] = jnp.zeros(q.shape, jnp.float32)

    def step(k, slot, final):
        nslot = 1 - slot
        a = jnp.broadcast_to(coef[0, k, 0:1, :], (Y, Z))
        b = jnp.broadcast_to(coef[1, k, 0:1, :], (Y, Z))
        for s in (1, 0):
            incoming = copies(slot, s)
            for c in incoming[2:]:
                c.wait()
            ay[:, s] = ay[:, s] + ry[slot, :, s]
            az[s] = az[s] + rz[slot, s]
            for xi in list(range(1, X - 1)) + [0, X - 1]:
                if xi == 0:
                    for c in incoming[:2]:
                        c.wait()
                    ax[:, s] = ax[:, s] + rx[slot, :, s]
                c, nb = near(lambda i: dbuf[slot, s, i], rx.at[slot], ry.at[slot], rz.at[slot], s, xi)
                summed = w_ref[0, xi] * (c - nb[0])
                for j in range(1, 6):
                    summed = summed + w_ref[j, xi] * (c - nb[j])
                xo[s][xi] = xo[s][xi] + c
                res = r_ref[s, xi] - (c + summed)
                r_ref[s, xi] = res
                if not final:
                    nd = a * c + b * res
                    dbuf[nslot, s, xi] = nd
                    put_faces(s, xi, nd)
            if not final:
                for c in copies(nslot, s):
                    c.start()

    def loop_step(k, carry):
        step(k, lax.rem(k, 2), False)
        return carry

    lax.fori_loop(0, CHEB - 1, loop_step, 0)
    step(CHEB - 1, (CHEB - 1) % 2, True)

    for xi in range(X):
        c0, n0 = near(lambda i: xo[0][i], ax, ay, az, 0, xi)
        c1, n1 = near(lambda i: xo[1][i], ax, ay, az, 1, xi)
        summed = (c0 - n0[0]) * (c1 - n1[0])
        for j in range(1, 6):
            summed = summed + (c0 - n0[j]) * (c1 - n1[j])
        g_ref[xi] = (-0.5 * time_step) * summed


def hand_over(*refs):
    n = len(refs) // 2
    for src, dst in zip(refs[:n], refs[n:]):
        dst[...] = src[...]


def body(conductivity, stored_state, row_scales, cotangent, upper_bound):
    X, Y, Z = conductivity.shape
    S = 2
    ngx = lax.axis_size("gx")
    ngy = lax.axis_size("gy")
    f32 = jnp.float32
    vmem = pl.BlockSpec(memory_space=pltpu.VMEM)
    field = jax.ShapeDtypeStruct((X, Y, Z), f32)
    results = pl.pallas_call(
        functools.partial(solve_kernel, ngx, ngy),
        out_shape=(field, field, field, jax.ShapeDtypeStruct((S, X, Y, Z), f32)),
        in_specs=[pl.BlockSpec(memory_space=pltpu.SMEM), vmem, vmem, vmem, vmem],
        out_specs=(vmem, vmem, vmem, vmem),
        scratch_shapes=[
            pltpu.VMEM((6, X, Y, Z), f32),
            pltpu.VMEM((X, Y, Z), stored_state.dtype),
            pltpu.VMEM((2, S, X, Y, Z), f32),
            pltpu.VMEM((2, S, Y, Z), f32),
            pltpu.VMEM((2, S, X, Z), f32),
            pltpu.VMEM((S, 2, X, Y), f32),
            pltpu.VMEM((2, 2, S, Y, Z), f32),
            pltpu.VMEM((2, 2, S, X, Z), f32),
            pltpu.VMEM((2, S, 2, X, Y), f32),
            pltpu.VMEM((2, S, Y, Z), f32),
            pltpu.VMEM((2, S, X, Z), f32),
            pltpu.VMEM((S, 2, X, Y), f32),
            pltpu.VMEM((2, CHEB, 8, Z), f32),
            pltpu.SemaphoreType.DMA((5, S, 2)),
            pltpu.SemaphoreType.DMA((5, S, 2)),
            pltpu.SemaphoreType.DMA((2,)),
        ],
        compiler_params=pltpu.CompilerParams(
            collective_id=0, has_side_effects=True, vmem_limit_bytes=60 * 1024 * 1024
        ),
    )(upper_bound, conductivity, stored_state, row_scales, cotangent)
    return pl.pallas_call(
        hand_over,
        out_shape=tuple(jax.ShapeDtypeStruct(o.shape, o.dtype) for o in results),
        in_specs=[vmem] * len(results),
        out_specs=tuple([vmem] * len(results)),
    )(*results)


def solution(mesh):
    return jax.shard_map(
        body,
        mesh=mesh,
        in_specs=(
            P("gx", "gy", "pa"),
            P("gx", "gy", "pa"),
            P("gx", "gy"),
            P("gx", "gy", "pa"),
            P(),
        ),
        out_specs=(
            P("gx", "gy", "pa"),
            P("gx", "gy", "pa"),
            P("gx", "gy", "pa"),
            P(None, "gx", "gy", "pa"),
        ),
        check_vma=False,
    )
```
